32 devices in a mesh: seg: 16 (over z, y, core), tp: 2 (over x).
Axes of the slice: x: 2, y: 2, z: 4, core: 2. Of those that a mesh axis runs over, the one named last changes fastest.
Arguments:
- tokens: bfloat16 [128, 4096], P('seg'), may hold values from -6 to 6
- w_query: bfloat16 [4096, 4096], P(None, 'tp'), may hold values from -0.09375 to 0.09375
- w_key: bfloat16 [4096, 1024], P(None, 'tp'), may hold values from -0.09375 to 0.09375
- w_value: bfloat16 [4096, 1024], P(None, 'tp'), may hold values from -0.09375 to 0.09375
- w_out: bfloat16 [4096, 4096], P('tp'), may hold values from -0.09375 to 0.09375
- gate_bias: float32 [32], P('tp'), may hold values from -3 to 3
- mem_store: float32 [256, 8, 128, 128], P('seg', 'tp'), may hold values from -6 to 6
- norm_store: float32 [256, 8, 128], P('seg', 'tp'), may hold values from 0.02 to 0.2
- k_cache: bfloat16 [128, 2048, 1024], P('seg', None, 'tp'), may hold values from -2500 to 2500
- v_cache: bfloat16 [128, 2048, 1024], P('seg', None, 'tp'), may hold values from -6 to 6
- home_owner: int32 [128], P('seg'), may hold values from 0 to 15, as said below
- home_slot: int32 [128], P('seg'), may hold values from 0 to 15
- cache_len: int32 [128], P('seg'), may hold values from 1 to 2048
- win_start: int32 [128], P('seg'), may hold values from 0 to 1023
Outputs:
- output: bfloat16 [128, 4096], P('seg', 'tp')
The draws below stay inside these ranges and needn't reach their ends.
Inputs may be any that keep to these rules, and one draw needn't show every extreme that they name: Request b's memory is row 16 * home_owner[b] + home_slot[b] of mem_store and norm_store; no two requests share a row, so one owner holds at most 16 requests, and some owner holds exactly 16.
All inputs are finite; a program needn't handle non-finite values.
Results may differ from the reference program's by a relative error of at most 0.0065.
The reference program's roundings to bfloat16 on the way (of `query`, `key_new`, `value_new`, `memory_read`, `probs` and `attended`) count: a program that leaves them out, or rounds other values in their place, can miss the bound.
Values may be sent and summed in bfloat16 or wider, within the bound.
No kernel may reach another device: no remote copies, remote signals or barrier semaphores. Data moves between devices by JAX's collectives and lax.ppermute only.
A program may use at most 128 MiB of HBM per device.

```python
import math
import jax
import jax.numpy as jnp
from jax import lax

D = 4096
H = 32
KVH = 8
DH = 128
WIN = 2048
SLOTS = 16
REQUESTS = 128
N_SEG = 16


def home_pairs(key):
    base_key = jax.random.fold_in(key, 7)
    key_hot, key_bias, key_score, key_order = jax.random.split(base_key, 4)
    slot_total = N_SEG * SLOTS
    global_row = jnp.arange(slot_total, dtype=jnp.int32)
    owner_of = global_row // SLOTS
    hottest = jax.random.randint(key_hot, (), 0, N_SEG)
    owner_bias = jax.random.randint(key_bias, (N_SEG,), 1, 4)
    at_ends = ((owner_of == 0) | (owner_of == N_SEG - 1)) & (global_row % SLOTS == 0)
    row_bias = jnp.where((owner_of == hottest) | at_ends, 0, owner_bias[owner_of])
    random_part = jax.random.randint(key_score, (slot_total,), 0, 65536)
    ranking = (row_bias * 65536 + random_part) * 1024 + global_row
    ordered = jnp.argsort(ranking, stable=True).astype(jnp.int32)
    chosen = ordered[:REQUESTS]
    shuffle = jax.random.permutation(key_order, REQUESTS)
    home_row = jnp.zeros((REQUESTS,), jnp.int32).at[shuffle].set(chosen)
    return ((home_row // SLOTS).astype(jnp.int32), (home_row % SLOTS).astype(jnp.int32))


def draw_home_owner(key, part):
    return home_pairs(key)[0]


def draw_home_slot(key, part):
    return home_pairs(key)[1]


def draw_k_cache(key, part):
    key_base = jax.random.fold_in(jax.random.fold_in(key, 11), 0)
    values = jax.random.normal(key_base, (REQUESTS, WIN, KVH * DH), jnp.float32)
    return values.astype(jnp.bfloat16)


def place_ends(values, rng, smallest, high):
    longest = values.shape.index(max(values.shape))
    spots = []
    for shift in (0, 1):
        where = [jax.random.randint(jax.random.fold_in(rng, axis), (), 0, length) for axis, length in enumerate(values.shape)]
        where[longest] = (where[longest] + shift) % values.shape[longest]
        spots.append(tuple(where))
    return values.at[spots[0]].set(smallest).at[spots[1]].set(high)


def steps_of(rng, dims, shards, smallest, top_value):
    loudness, own = 1.0, jax.random.fold_in(rng, 6)
    for dim, parts in shards:
        draws = jnp.exp(jax.random.uniform(jax.random.fold_in(own, dim), (parts,), jnp.float32, smallest / len(shards), top_value / len(shards)))
        loudness = loudness * jnp.repeat(draws, dims[dim] // parts).reshape([-1 if axis == dim else 1 for axis in range(len(dims))])
    return loudness


def scatter_about(key, extent, width, limit, cuts=(), kind=jnp.bfloat16):
    loudness = steps_of(key, extent, cuts, -0.22, 0.18) if cuts else 1.0
    values = jax.random.normal(key, extent, jnp.float32) * width * loudness
    return jnp.minimum(jnp.maximum(values, -limit), limit).astype(kind)


def setup_inputs(seed: int = 0) -> dict:
    keys = jax.random.split(jax.random.key(seed), 15)
    tokens = scatter_about(keys[0], (REQUESTS, D), 1.0, 6.0, ((0, 16),))
    w_query = scatter_about(keys[1], (D, H * DH), D ** -0.5, 0.09375, ((1, 2),))
    w_key = scatter_about(keys[2], (D, KVH * DH), D ** -0.5, 0.09375, ((1, 2),))
    w_value = scatter_about(keys[3], (D, KVH * DH), D ** -0.5, 0.09375, ((1, 2),))
    w_out = scatter_about(keys[4], (H * DH, D), (H * DH) ** -0.5, 0.09375, ((0, 2),))
    gate_bias = jnp.clip(jax.random.uniform(keys[5], (H,), jnp.float32, -3.0, 3.0) * steps_of(keys[5], (H,), ((0, 2),), -0.4, 0.0), -3.0, 3.0)
    mem_store = scatter_about(keys[6], (N_SEG * SLOTS, KVH, DH, DH), 1.0, 6.0, ((0, 16), (1, 2)), jnp.float32)
    norm_store = jnp.clip(jnp.exp(math.log(0.2) - 2.3025851 * jax.random.uniform(keys[7], (N_SEG * SLOTS, KVH, DH), jnp.float32) ** steps_of(keys[7], (N_SEG * SLOTS, KVH, DH), ((0, 16), (1, 2)), -0.2, 0.2)), 0.02, 0.2)
    k_cache = draw_k_cache(jax.random.fold_in(keys[14], 71), 0)
    v_cache = scatter_about(keys[9], (REQUESTS, WIN, KVH * DH), 1.0, 6.0, ((0, 16), (2, 2)))
    home_owner = draw_home_owner(jax.random.fold_in(keys[14], 71), 0)
    home_slot = draw_home_slot(jax.random.fold_in(keys[14], 71), 0)
    cache_len = place_ends(jax.random.randint(keys[12], (REQUESTS,), 1, WIN + 1), jax.random.fold_in(keys[12], 1), 1, WIN).astype(jnp.int32)
    win_start = place_ends(jax.random.randint(keys[13], (REQUESTS,), 0, WIN // 2), jax.random.fold_in(keys[13], 1), 0, (WIN // 2) - 1).astype(jnp.int32)
    return {"tokens": tokens, "w_query": w_query, "w_key": w_key, "w_value": w_value, "w_out": w_out, "gate_bias": gate_bias, "mem_store": mem_store, "norm_store": norm_store, "k_cache": k_cache, "v_cache": v_cache, "home_owner": home_owner, "home_slot": home_slot, "cache_len": cache_len, "win_start": win_start}


def elu_plus(values):
    return jnp.where(values > 0, values + 1.0, jnp.exp(jnp.minimum(values, 0.0)))


def reference(tokens, w_query, w_key, w_value, w_out, gate_bias, mem_store, norm_store, k_cache, v_cache, home_owner, home_slot, cache_len, win_start):
    group_size = H // KVH
    query = jnp.dot(tokens, w_query, preferred_element_type=jnp.float32).astype(jnp.bfloat16)
    key_new = jnp.dot(tokens, w_key, preferred_element_type=jnp.float32).astype(jnp.bfloat16)
    value_new = jnp.dot(tokens, w_value, preferred_element_type=jnp.float32).astype(jnp.bfloat16)
    query_heads = query.astype(jnp.float32).reshape(REQUESTS, KVH, group_size, DH)
    lifted = elu_plus(query_heads)
    home_row = (home_owner * SLOTS + home_slot).astype(jnp.int32)
    picked = jnp.take(mem_store, home_row, axis=0)
    normed = jnp.take(norm_store, home_row, axis=0)
    numerator = jnp.einsum('bkgi,bkij->bkgj', lifted, picked, precision=lax.Precision.HIGHEST)
    denominator = jnp.einsum('bkgi,bki->bkg', lifted, normed, precision=lax.Precision.HIGHEST)
    memory_read = lax.optimization_barrier((numerator / denominator[..., None]).astype(jnp.bfloat16))
    memory_read = memory_read.astype(jnp.float32)
    score_scale = DH ** -0.5
    cache_keys = k_cache.astype(jnp.float32).reshape(REQUESTS, WIN, KVH, DH)
    cache_values = v_cache.astype(jnp.float32).reshape(REQUESTS, WIN, KVH, DH)
    scores = jnp.einsum('bkgi,bjki->bkgj', query_heads, cache_keys) * score_scale
    own_key = key_new.astype(jnp.float32).reshape(REQUESTS, KVH, DH)
    own_score = jnp.einsum('bkgi,bki->bkg', query_heads, own_key) * score_scale
    position = jnp.arange(WIN, dtype=jnp.int32)
    live_mask = (position[None, :] >= win_start[:, None]) & (position[None, :] < cache_len[:, None])
    live_four = live_mask[:, None, None, :]
    top_score = jnp.maximum(jnp.max(jnp.where(live_four, scores, -jnp.inf), axis=-1), own_score)
    weights = jnp.where(live_four, jnp.exp(scores - top_score[..., None]), 0.0)
    own_weight = jnp.exp(own_score - top_score)
    softmax_total = jnp.sum(weights, axis=-1) + own_weight
    probs = (weights / softmax_total[..., None]).astype(jnp.bfloat16)
    own_prob = (own_weight / softmax_total).astype(jnp.bfloat16)
    local_read = jnp.einsum('bkgj,bjki->bkgi', probs.astype(jnp.float32), cache_values)
    own_value = value_new.astype(jnp.float32).reshape(REQUESTS, KVH, 1, DH)
    local_read = local_read + own_prob.astype(jnp.float32)[..., None] * own_value
    mix_gate = jax.nn.sigmoid(gate_bias).reshape(KVH, group_size)[None, :, :, None]
    attended = (mix_gate * memory_read + (1.0 - mix_gate) * local_read).astype(jnp.bfloat16)
    attended = attended.reshape(REQUESTS, H * DH)
    return jnp.dot(attended, w_out, preferred_element_type=jnp.float32).astype(jnp.bfloat16)
```

```python
import functools

import jax
import jax.numpy as jnp
from jax import lax
from jax.experimental import pallas as pl
from jax.experimental.pallas import tpu as pltpu
from jax.sharding import PartitionSpec as P

DH = 128
MIB = 2**20
BF = jnp.bfloat16
F32 = jnp.float32

ANY = pl.BlockSpec(memory_space=pl.ANY)
VM = pl.BlockSpec(memory_space=pltpu.VMEM)
HBM = pl.BlockSpec(memory_space=pltpu.HBM)


def call(kernel, name, out_shape, in_specs, scratch, mib, flops, nbytes, args):
    many = isinstance(out_shape, (list, tuple))
    args = [
        pltpu.with_memory_space_constraint(a, pltpu.HBM) if spec is HBM else a
        for a, spec in zip(args, in_specs)
    ]
    return pl.pallas_call(
        kernel,
        name=name,
        out_shape=out_shape,
        in_specs=in_specs,
        out_specs=[VM] * len(out_shape) if many else VM,
        scratch_shapes=scratch,
        compiler_params=pltpu.CompilerParams(vmem_limit_bytes=mib * MIB),
        cost_estimate=pl.CostEstimate(flops=flops, bytes_accessed=nbytes, transcendentals=0),
    )(*args)


def elu_plus(values):
    return jnp.where(values > 0, values + 1.0, jnp.exp(jnp.minimum(values, 0.0)))


def fetch_all(pairs, sems):
    copies = [pltpu.make_async_copy(a, b, sems.at[i]) for i, (a, b) in enumerate(pairs)]
    for c in copies:
        c.start()
    return copies


def query_kernel(owner_hbm, slot_hbm, x_hbm, w_ref, q_ref, qh_ref, owner_ref, slot_ref, x_ref,
                 buf, sems, small):
    rows, cols = x_ref.shape[0], w_ref.shape[1]
    count, depth = buf.shape[0], buf.shape[1]

    def copy(i):
        return pltpu.make_async_copy(w_ref.at[pl.ds(i * depth, depth), :], buf.at[i], sems.at[i])

    first = fetch_all([(x_hbm, x_ref), (owner_hbm, owner_ref), (slot_hbm, slot_ref)], small)
    for i in range(count):
        copy(i).start()
    for c in first:
        c.wait()
    row = lax.broadcasted_iota(jnp.int32, (rows, DH), 0)
    lane = lax.broadcasted_iota(jnp.int32, (rows, DH), 1)
    extra = jnp.zeros((rows, DH), F32)
    for r in range(rows):
        extra = jnp.where((row == r) & (lane == 0), owner_ref[r].astype(F32), extra)
        extra = jnp.where((row == r) & (lane == 1), slot_ref[r].astype(F32), extra)
    q_ref[:, cols:] = extra.astype(BF)
    total = jnp.zeros((rows, cols), F32)
    for i in range(count):
        copy(i).wait()
        total = total + jnp.dot(
            x_ref[:, i * depth : (i + 1) * depth], buf[i], preferred_element_type=F32
        )
    query = total.astype(BF)
    q_ref[:, :cols] = query
    wide = query.astype(F32)
    for h in range(cols // DH):
        qh_ref[:, h, :] = wide[:, h * DH : (h + 1) * DH]


def keyval_kernel(x_hbm, wk_ref, wv_ref, k_ref, v_ref, x_ref, bufk, bufv, sems, small):
    count, depth = bufk.shape[0], bufk.shape[1]

    def copies(i):
        at = pl.ds(i * depth, depth)
        return (
            pltpu.make_async_copy(wk_ref.at[at, :], bufk.at[i], sems.at[0, i]),
            pltpu.make_async_copy(wv_ref.at[at, :], bufv.at[i], sems.at[1, i]),
        )

    first = fetch_all([(x_hbm, x_ref)], small)
    for i in range(count):
        for c in copies(i):
            c.start()
    first[0].wait()
    key = jnp.zeros(k_ref.shape, F32)
    val = jnp.zeros(v_ref.shape, F32)
    for i in range(count):
        for c in copies(i):
            c.wait()
        part = x_ref[:, i * depth : (i + 1) * depth]
        key = key + jnp.dot(part, bufk[i], preferred_element_type=F32)
        val = val + jnp.dot(part, bufv[i], preferred_element_type=F32)
    k_ref[...] = key.astype(BF)
    v_ref[...] = val.astype(BF)


def live_blocks(start_ref, len_ref, r, block):
    lo = start_ref[r] // block
    hi = (len_ref[r] + block - 1) // block
    return lo, jnp.maximum(hi, lo)


def probs_kernel(len_hbm, start_hbm, qh_ref, kn_ref, kc_ref, p_ref, own_ref, len_ref, start_ref,
                 buf, score, sems, small):
    rows, heads, window = p_ref.shape
    kv = kc_ref.shape[2] // DH
    group = heads // kv
    block = window // 8

    def copy(r, b):
        at = pl.ds(pl.multiple_of(b * block, block), block)
        return pltpu.make_async_copy(kc_ref.at[r, at, :], buf.at[r, at, :], sems.at[r])

    for c in fetch_all([(len_hbm, len_ref), (start_hbm, start_ref)], small):
        c.wait()
    for r in range(rows):
        lo, hi = live_blocks(start_ref, len_ref, r, block)
        lax.fori_loop(lo, hi, lambda b, c: (copy(r, b).start(), c)[1], 0)
    which = lax.broadcasted_iota(jnp.int32, (heads, DH), 0) // group
    scale = DH ** (-0.5)
    for r in range(rows):
        q = qh_ref[r]
        wide = jnp.concatenate([jnp.where(which == k, q, 0.0) for k in range(kv)], axis=1)
        lo, hi = live_blocks(start_ref, len_ref, r, block)
        lax.fori_loop(lo, hi, lambda b, c: (copy(r, b).wait(), c)[1], 0)
        score[r] = (
            lax.dot_general(
                wide.astype(BF), buf[r], (((1,), (1,)), ((), ())), preferred_element_type=F32
            )
            * scale
        )
    position = lax.broadcasted_iota(jnp.int32, (heads, window), 1)
    for r in range(rows):
        q = qh_ref[r]
        key = jnp.zeros((heads, DH), F32)
        for k in range(kv):
            one = kn_ref[r : r + 1, k * DH : (k + 1) * DH].astype(F32)
            key = jnp.where(which == k, one, key)
        own = jnp.sum(q * key, axis=1, keepdims=True) * scale
        live = (position >= start_ref[r]) & (position < len_ref[r])
        s = jnp.where(live, score[r], -jnp.inf)
        top = jnp.maximum(jnp.max(s, axis=1, keepdims=True), own)
        weight = jnp.exp(s - top)
        own_weight = jnp.exp(own - top)
        inverse = 1.0 / (jnp.sum(weight, axis=1, keepdims=True) + own_weight)
        p_ref[r] = (weight * inverse).astype(BF)
        prob = (own_weight * inverse).astype(BF).astype(F32)
        own_ref[r] = jnp.broadcast_to(prob, (heads, DH))


def values_kernel(len_hbm, start_hbm, p_ref, own_ref, vn_ref, vc_ref, out_ref, len_ref, start_ref,
                  buf, sems, small):
    rows, heads, window = p_ref.shape
    kv = vc_ref.shape[2] // DH
    group = heads // kv
    block = window // 8

    def copy(r, b):
        at = pl.ds(pl.multiple_of(b * block, block), block)
        return pltpu.make_async_copy(vc_ref.at[r, at, :], buf.at[r, at, :], sems.at[r])

    for c in fetch_all([(len_hbm, len_ref), (start_hbm, start_ref)], small):
        c.wait()
    for r in range(rows):
        lo, hi = live_blocks(start_ref, len_ref, r, block)
        lax.fori_loop(lo, hi, lambda b, c: (copy(r, b).start(), c)[1], 0)
    nothing = jnp.zeros((block, kv * DH), BF)

    def clear(r, b, c):
        buf[r, pl.ds(pl.multiple_of(b * block, block), block), :] = nothing
        return c

    which = lax.broadcasted_iota(jnp.int32, (heads, DH), 0) // group
    for r in range(rows):
        lo, hi = live_blocks(start_ref, len_ref, r, block)
        lax.fori_loop(0, lo, functools.partial(clear, r), 0)
        lax.fori_loop(hi, window // block, functools.partial(clear, r), 0)
    for r in range(rows):
        lo, hi = live_blocks(start_ref, len_ref, r, block)
        lax.fori_loop(lo, hi, lambda b, c: (copy(r, b).wait(), c)[1], 0)
        every = jnp.dot(p_ref[r], buf[r], preferred_element_type=F32)
        read = jnp.zeros((heads, DH), F32)
        for k in range(kv):
            at = slice(k * DH, (k + 1) * DH)
            value = vn_ref[r : r + 1, at].astype(F32)
            read = jnp.where(which == k, every[:, at] + own_ref[r] * value, read)
        out_ref[r] = read


def route_kernel(cols, slots, *refs):
    *row_refs, mine_ref, other_ref, sel_ref = refs
    me = lax.axis_index("seg")
    half = lax.rem(me, 2)
    first = me - half
    rows = jnp.concatenate([r[...] for r in row_refs], axis=0)
    owner = rows[:, cols : cols + 1].astype(F32).astype(jnp.int32)
    slot = rows[:, cols + 1 : cols + 2].astype(F32).astype(jnp.int32)
    rel = owner - first
    near = (rel >= 0) & (rel < 2)
    target = jnp.where(rel == half, 0, slots) + slot
    target = jnp.where(near, target, -1)
    lane = lax.broadcasted_iota(jnp.int32, (rows.shape[0], 2 * slots), 1)
    sel = (lane == target).astype(F32).astype(BF)
    sel_ref[...] = sel
    picked = lax.dot_general(
        sel, rows[:, :cols], (((0,), (0,)), ((), ())), preferred_element_type=F32
    ).astype(BF)
    mine_ref[...] = picked[:slots]
    other_ref[...] = picked[slots:]


def readout_kernel(mine_ref, got_ref, norm_hbm, mem_ref, out_ref, norm_ref, buf, lift, read, sems,
                   small):
    slots, kv = mem_ref.shape[0], mem_ref.shape[1]
    cols = mine_ref.shape[1]
    heads = cols // DH
    group = heads // kv
    first = fetch_all([(norm_hbm, norm_ref)], small)
    for t in range(slots):
        pltpu.make_async_copy(mem_ref.at[t], buf.at[t], sems.at[t]).start()
    lifted = elu_plus(mine_ref[...].astype(F32) + got_ref[...].astype(F32))
    for h in range(heads):
        lift[:, h, :] = lifted[:, h * DH : (h + 1) * DH]
    which = lax.broadcasted_iota(jnp.int32, (heads, DH), 0) // group
    first[0].wait()
    for t in range(slots):
        row = lift[t]
        norm = jnp.zeros((heads, DH), F32)
        for k in range(kv):
            norm = jnp.where(which == k, norm_ref[t, k : k + 1, :], norm)
        denom = jnp.sum(row * norm, axis=1, keepdims=True)
        high = row.astype(BF).astype(F32)
        both = jnp.concatenate([high, row - high], axis=0)
        same = jnp.concatenate([which, which], axis=0)
        wide = jnp.concatenate([jnp.where(same == k, both, 0.0) for k in range(kv)], axis=1)
        wide = wide.astype(BF)
        pltpu.make_async_copy(mem_ref.at[t], buf.at[t], sems.at[t]).wait()
        mem = buf[t].reshape(kv * DH, DH)
        mem_high = mem.astype(BF)
        mem_low = (mem - mem_high.astype(F32)).astype(BF)
        top = jnp.dot(wide, mem_high, preferred_element_type=F32)
        low = jnp.dot(wide, mem_low, preferred_element_type=F32)
        numer = top[:heads] + (top[heads:] + low[:heads])
        read[t] = (numer / denom).astype(BF).astype(F32)
    for h in range(heads):
        out_ref[:, h * DH : (h + 1) * DH] = read[:, h, :].astype(BF)


def spread_kernel(sel_ref, mine_ref, other_ref, *out_refs):
    reads = jnp.concatenate([mine_ref[...], other_ref[...]], axis=0)
    rows = out_refs[0].shape[0]
    every = jnp.dot(sel_ref[...], reads, preferred_element_type=F32).astype(BF)
    for i, out in enumerate(out_refs):
        out[...] = every[i * rows : (i + 1) * rows]


def fetch_kernel(w_ref, out_ref, sems):
    count = sems.shape[0]
    depth = w_ref.shape[0] // count

    def copy(i):
        at = pl.ds(i * depth, depth)
        return pltpu.make_async_copy(w_ref.at[at, :], out_ref.at[at, :], sems.at[i])

    for i in range(count):
        copy(i).start()
    for i in range(count):
        copy(i).wait()


def columns_of(w_ref, tp, j):
    cols = w_ref.shape[1] // tp
    first = lax.rem(lax.axis_index("tp") + j, tp) * cols
    return w_ref[:, pl.ds(pl.multiple_of(first, DH), cols)]


def away_kernel(tp, gate_hbm, kept_ref, got_ref, local_ref, w_ref, out_ref, att_ref, gate_ref, small):
    heads = local_ref.shape[1]
    for c in fetch_all([(gate_hbm, gate_ref)], small):
        c.wait()
    gate = jax.nn.sigmoid(gate_ref[...])
    for h in range(heads):
        at = slice(h * DH, (h + 1) * DH)
        memory = kept_ref[:, at].astype(F32) + got_ref[:, at].astype(F32)
        mix = gate[:, h : h + 1]
        att_ref[:, at] = (mix * memory + (1.0 - mix) * local_ref[:, h, :]).astype(BF)
    for j in range(1, tp):
        out_ref[j - 1] = jnp.dot(
            att_ref[...], columns_of(w_ref, tp, j), preferred_element_type=F32
        )


def home_kernel(tp, att_ref, w_ref, out_ref):
    out_ref[...] = jnp.dot(att_ref[...], columns_of(w_ref, tp, 0), preferred_element_type=F32)


def body(seg, tp, tokens, w_query, w_key, w_value, w_out, gate_bias, mem_store, norm_store,
         k_cache, v_cache, home_owner, home_slot, cache_len, win_start):
    rows, width = tokens.shape
    cols = w_query.shape[1]
    heads = cols // DH
    window = k_cache.shape[1]
    kv_cols = k_cache.shape[2]
    kv = kv_cols // DH
    slots = mem_store.shape[0]
    chips = seg // 2
    zs = chips // 2
    sds = jax.ShapeDtypeStruct
    dma = pltpu.SemaphoreType.DMA

    def swap(value, mask):
        return lax.ppermute(value, "seg", [(i, i ^ mask) for i in range(seg)])

    q_blocks = 16
    query, query_heads = call(
        query_kernel, "query",
        [sds((rows, cols + DH), BF), sds((rows, heads, DH), F32)],
        [HBM] * 4,
        [pltpu.SMEM((rows,), jnp.int32)] * 2
        + [pltpu.VMEM((rows, width), BF),
           pltpu.VMEM((q_blocks, width // q_blocks, cols), BF), dma((q_blocks,)), dma((3,))],
        24, 2 * rows * width * cols, 2 * width * cols,
        (home_owner, home_slot, tokens, w_query),
    )
    near = swap(query, 2)
    kv_blocks = 8
    key_new, value_new = call(
        keyval_kernel, "keyval",
        [sds((rows, kv_cols), BF)] * 2,
        [HBM, ANY, ANY],
        [pltpu.VMEM((rows, width), BF)]
        + [pltpu.VMEM((kv_blocks, width // kv_blocks, kv_cols), BF)] * 2
        + [dma((2, kv_blocks)), dma((1,))],
        12, 4 * rows * width * kv_cols, 4 * width * kv_cols,
        (tokens, w_key, w_value),
    )
    near, key_new, value_new = lax.optimization_barrier((near, key_new, value_new))
    pair = jnp.concatenate([query, near], axis=0)
    far = [swap(pair, 4 * j) for j in range(1, zs)]
    probs, own_prob = call(
        probs_kernel, "probs",
        [sds((rows, heads, window), BF), sds((rows, heads, DH), F32)],
        [HBM, HBM, VM, VM, HBM],
        [pltpu.SMEM((rows,), jnp.int32)] * 2
        + [pltpu.VMEM((rows, window, kv_cols), BF), pltpu.VMEM((rows, heads, window), F32),
           dma((rows,)), dma((2,))],
        20, 2 * rows * heads * window * kv_cols, rows * window * kv_cols,
        (cache_len, win_start, query_heads, key_new, k_cache),
    )
    far, probs, own_prob = lax.optimization_barrier((far, probs, own_prob))
    mine, other, sel = call(
        functools.partial(route_kernel, cols, slots), "route",
        [sds((slots, cols), BF)] * 2 + [sds((chips * rows, 2 * slots), BF)],
        [VM] * zs, [], 8, 4 * slots * chips * rows * cols, 0,
        (pair, *far),
    )
    got = swap(other, 1)
    read = call(
        readout_kernel, "readout",
        sds((slots, cols), BF),
        [VM, VM, HBM, ANY],
        [pltpu.VMEM((slots, kv, DH), F32), pltpu.VMEM((slots, kv, DH, DH), F32)]
        + [pltpu.VMEM((slots, heads, DH), F32)] * 2 + [dma((slots,)), dma((1,))],
        8, 8 * slots * heads * DH * DH, 4 * slots * kv * DH * DH,
        (mine, got, norm_store, mem_store),
    )
    partner = swap(read, 1)
    here, *away = call(
        spread_kernel, "spread",
        [sds((2 * rows, cols), BF)] * zs,
        [VM] * 3, [], 8, 4 * slots * chips * rows * cols, 0,
        (sel, read, partner),
    )
    back = [swap(away[j - 1], 4 * j) for j in range(1, zs)]
    away, probs = lax.optimization_barrier((away, probs))
    local_read = call(
        values_kernel, "values",
        sds((rows, heads, DH), F32),
        [HBM, HBM, VM, VM, VM, HBM],
        [pltpu.SMEM((rows,), jnp.int32)] * 2
        + [pltpu.VMEM((rows, window, kv_cols), BF), dma((rows,)), dma((2,))],
        18, 2 * rows * heads * window * kv_cols, rows * window * kv_cols,
        (cache_len, win_start, probs, own_prob, value_new, v_cache),
    )
    back, local_read = lax.optimization_barrier((back, local_read))
    for value in back:
        here = here + value
    kept, leaving = here[:rows], here[rows:]
    last = swap(leaving, 2)
    w_fast = call(
        fetch_kernel, "fetch",
        sds(w_out.shape, BF), [ANY], [dma((16,))],
        4, 0, 2 * w_out.shape[0] * w_out.shape[1],
        (w_out,),
    )
    last, w_fast = lax.optimization_barrier((last, w_fast))
    out_cols = w_out.shape[1] // tp
    others, attended = call(
        functools.partial(away_kernel, tp), "away",
        [sds((tp - 1, rows, out_cols), F32), sds((rows, cols), BF)],
        [HBM, VM, VM, VM, VM], [pltpu.VMEM((1, heads), F32), dma((1,))],
        4, 2 * rows * cols * (w_out.shape[1] - out_cols), 0,
        (gate_bias.reshape(1, heads), kept, last, local_read, w_fast),
    )
    came = [
        lax.ppermute(others[j - 1], "tp", [(i, (i + j) % tp) for i in range(tp)])
        for j in range(1, tp)
    ]
    result = call(
        functools.partial(home_kernel, tp), "home",
        sds((rows, out_cols), F32), [VM, VM], [],
        4, 2 * rows * cols * out_cols, 0,
        (attended, w_fast),
    )
    came, result = lax.optimization_barrier((came, result))
    for value in came:
        result = result + value
    return result.astype(BF)


def solution(mesh):
    placed = (
        P("seg", None),
        P(None, "tp"),
        P(None, "tp"),
        P(None, "tp"),
        P("tp", None),
        P("tp"),
        P("seg", "tp", None, None),
        P("seg", "tp", None),
        P("seg", None, "tp"),
        P("seg", None, "tp"),
        P("seg"),
        P("seg"),
        P("seg"),
        P("seg"),
    )
    inner = functools.partial(body, mesh.shape["seg"], mesh.shape["tp"])
    return jax.shard_map(
        inner, mesh=mesh, in_specs=placed, out_specs=P("seg", "tp"), check_vma=False
    )
```

```python
import functools

import jax
import jax.numpy as jnp
from jax import lax
from jax.experimental import pallas as pl
from jax.experimental.pallas import tpu as pltpu
from jax.sharding import PartitionSpec as P

DH = 128
MIB = 2**20
BF = jnp.bfloat16
F32 = jnp.float32

ANY = pl.BlockSpec(memory_space=pl.ANY)
VM = pl.BlockSpec(memory_space=pltpu.VMEM)
HBM = pl.BlockSpec(memory_space=pltpu.HBM)


def call(kernel, name, out_shape, in_specs, scratch, mib, flops, nbytes, args):
    many = isinstance(out_shape, (list, tuple))
    args = [
        pltpu.with_memory_space_constraint(a, pltpu.HBM) if spec is HBM else a
        for a, spec in zip(args, in_specs)
    ]
    return pl.pallas_call(
        kernel,
        name=name,
        out_shape=out_shape,
        in_specs=in_specs,
        out_specs=[VM] * len(out_shape) if many else VM,
        scratch_shapes=scratch,
        compiler_params=pltpu.CompilerParams(vmem_limit_bytes=mib * MIB),
        cost_estimate=pl.CostEstimate(flops=flops, bytes_accessed=nbytes, transcendentals=0),
    )(*args)


def elu_plus(values):
    return jnp.where(values > 0, values + 1.0, jnp.exp(jnp.minimum(values, 0.0)))


def fetch_all(pairs, sems):
    copies = [pltpu.make_async_copy(a, b, sems.at[i]) for i, (a, b) in enumerate(pairs)]
    for c in copies:
        c.start()
    return copies


def query_kernel(owner_hbm, slot_hbm, x_hbm, w_ref, q_ref, qh_ref, owner_ref, slot_ref, x_ref,
                 buf, sems, small):
    rows, cols = x_ref.shape[0], w_ref.shape[1]
    count, depth = buf.shape[0], buf.shape[1]

    def copy(i):
        return pltpu.make_async_copy(w_ref.at[pl.ds(i * depth, depth), :], buf.at[i], sems.at[i])

    first = fetch_all([(x_hbm, x_ref), (owner_hbm, owner_ref), (slot_hbm, slot_ref)], small)
    for i in range(count):
        copy(i).start()
    for c in first:
        c.wait()
    row = lax.broadcasted_iota(jnp.int32, (rows, DH), 0)
    lane = lax.broadcasted_iota(jnp.int32, (rows, DH), 1)
    extra = jnp.zeros((rows, DH), F32)
    for r in range(rows):
        extra = jnp.where((row == r) & (lane == 0), owner_ref[r].astype(F32), extra)
        extra = jnp.where((row == r) & (lane == 1), slot_ref[r].astype(F32), extra)
    q_ref[:, cols:] = extra.astype(BF)
    total = jnp.zeros((rows, cols), F32)
    for i in range(count):
        copy(i).wait()
        total = total + jnp.dot(
            x_ref[:, i * depth : (i + 1) * depth], buf[i], preferred_element_type=F32
        )
    query = total.astype(BF)
    q_ref[:, :cols] = query
    wide = query.astype(F32)
    for h in range(cols // DH):
        qh_ref[:, h, :] = wide[:, h * DH : (h + 1) * DH]


def keyval_kernel(x_hbm, wk_ref, wv_ref, k_ref, v_ref, x_ref, bufk, bufv, sems, small):
    count, depth = bufk.shape[0], bufk.shape[1]

    def copies(i):
        at = pl.ds(i * depth, depth)
        return (
            pltpu.make_async_copy(wk_ref.at[at, :], bufk.at[i], sems.at[0, i]),
            pltpu.make_async_copy(wv_ref.at[at, :], bufv.at[i], sems.at[1, i]),
        )

    first = fetch_all([(x_hbm, x_ref)], small)
    for i in range(count):
        for c in copies(i):
            c.start()
    first[0].wait()
    key = jnp.zeros(k_ref.shape, F32)
    val = jnp.zeros(v_ref.shape, F32)
    for i in range(count):
        for c in copies(i):
            c.wait()
        part = x_ref[:, i * depth : (i + 1) * depth]
        key = key + jnp.dot(part, bufk[i], preferred_element_type=F32)
        val = val + jnp.dot(part, bufv[i], preferred_element_type=F32)
    k_ref[...] = key.astype(BF)
    v_ref[...] = val.astype(BF)


def live_blocks(start_ref, len_ref, r):
    lo = start_ref[r] // DH
    return lo, jnp.maximum((len_ref[r] + DH - 1) // DH - lo, 0)


def each_copy(cache_ref, buf, sems, r, lo, count, act):
    size = 1
    while size < buf.shape[1] // DH:
        size *= 2
    while size:
        here, now = lo, size

        @pl.when((count & now) != 0)
        def _():
            at = pl.ds(pl.multiple_of(here * DH, DH), now * DH)
            act(pltpu.make_async_copy(cache_ref.at[r, at, :], buf.at[r, at, :], sems.at[r]))

        lo = lo + (count & size)
        size //= 2


def by_length(window, lo, count, step, act):
    need = (count * DH + step - 1) // step
    for n in range(1, window // step + 1):
        first = pl.multiple_of(jnp.minimum(lo * DH, window - n * step), DH)
        pl.when(need == n)(functools.partial(act, first, n * step))


def probs_kernel(len_hbm, start_hbm, qh_ref, kn_ref, kc_ref, p_ref, own_ref, len_ref, start_ref,
                 buf, score, wide_ref, sems, small):
    rows, heads, window = p_ref.shape
    kv = kc_ref.shape[2] // DH
    group = heads // kv
    for c in fetch_all([(len_hbm, len_ref), (start_hbm, start_ref)], small):
        c.wait()

    @pl.loop(0, rows)
    def _(r):
        lo, count = live_blocks(start_ref, len_ref, r)
        each_copy(kc_ref, buf, sems, r, lo, count, lambda c: c.start())

    which = lax.broadcasted_iota(jnp.int32, (heads, DH), 0) // group
    scale = DH ** (-0.5)
    for r in range(rows):
        q = qh_ref[r]
        for k in range(kv):
            wide_ref[r, :, k * DH : (k + 1) * DH] = jnp.where(which == k, q, 0.0).astype(BF)

    @pl.loop(0, rows)
    def _(r):
        lo, count = live_blocks(start_ref, len_ref, r)
        each_copy(kc_ref, buf, sems, r, lo, count, lambda c: c.wait())

        def product(first, size):
            at = pl.ds(first, size)
            score[r, :, at] = lax.dot_general(
                wide_ref[r], buf[r, at, :], (((1,), (1,)), ((), ())), preferred_element_type=F32
            )

        by_length(window, lo, count, window // 4, product)

    position = lax.broadcasted_iota(jnp.int32, (heads, window), 1)
    for r in range(rows):
        q = qh_ref[r]
        key = jnp.zeros((heads, DH), F32)
        for k in range(kv):
            one = kn_ref[r : r + 1, k * DH : (k + 1) * DH].astype(F32)
            key = jnp.where(which == k, one, key)
        own = jnp.sum(q * key, axis=1, keepdims=True) * scale
        live = (position >= start_ref[r]) & (position < len_ref[r])
        s = jnp.where(live, score[r] * scale, -jnp.inf)
        top = jnp.maximum(jnp.max(s, axis=1, keepdims=True), own)
        weight = jnp.exp(s - top)
        own_weight = jnp.exp(own - top)
        inverse = 1.0 / (jnp.sum(weight, axis=1, keepdims=True) + own_weight)
        p_ref[r] = (weight * inverse).astype(BF)
        prob = (own_weight * inverse).astype(BF).astype(F32)
        own_ref[r] = jnp.broadcast_to(prob, (heads, DH))


def values_kernel(len_hbm, start_hbm, p_ref, own_ref, vn_ref, vc_ref, out_ref, len_ref, start_ref,
                  buf, sems, small):
    rows, heads, window = p_ref.shape
    kv = vc_ref.shape[2] // DH
    group = heads // kv
    for c in fetch_all([(len_hbm, len_ref), (start_hbm, start_ref)], small):
        c.wait()

    @pl.loop(0, rows)
    def _(r):
        lo, count = live_blocks(start_ref, len_ref, r)
        each_copy(vc_ref, buf, sems, r, lo, count, lambda c: c.start())

    which = lax.broadcasted_iota(jnp.int32, (heads, DH), 0) // group
    nothing = jnp.zeros((DH, kv * DH), BF)

    @pl.loop(0, rows)
    def _(r):
        lo, count = live_blocks(start_ref, len_ref, r)
        base = jnp.zeros((heads, DH), F32)
        for k in range(kv):
            value = vn_ref[r, :, k * DH : (k + 1) * DH].astype(F32)
            base = jnp.where(which == k, own_ref[r] * value, base)
        out_ref[r] = base

        def clear(b):
            buf[r, pl.ds(pl.multiple_of(b * DH, DH), DH), :] = nothing

        def product(first, size):
            pl.loop(first // DH, lo)(clear)
            pl.loop(lo + count, (first + size) // DH)(clear)
            each_copy(vc_ref, buf, sems, r, lo, count, lambda c: c.wait())
            at = pl.ds(first, size)
            every = jnp.dot(p_ref[r, :, at], buf[r, at, :], preferred_element_type=F32)
            read = jnp.zeros((heads, DH), F32)
            for k in range(kv):
                read = jnp.where(which == k, every[:, k * DH : (k + 1) * DH], read)
            out_ref[r] += read

        by_length(window, lo, count, window // 4, product)


def route_kernel(cols, slots, *refs):
    *row_refs, mine_ref, other_ref, sel_ref = refs
    me = lax.axis_index("seg")
    half = lax.rem(me, 2)
    first = me - half
    rows = jnp.concatenate([r[...] for r in row_refs], axis=0)
    owner = rows[:, cols : cols + 1].astype(F32).astype(jnp.int32)
    slot = rows[:, cols + 1 : cols + 2].astype(F32).astype(jnp.int32)
    rel = owner - first
    near = (rel >= 0) & (rel < 2)
    target = jnp.where(rel == half, 0, slots) + slot
    target = jnp.where(near, target, -1)
    lane = lax.broadcasted_iota(jnp.int32, (rows.shape[0], 2 * slots), 1)
    sel = (lane == target).astype(F32).astype(BF)
    sel_ref[...] = sel
    picked = lax.dot_general(
        sel, rows[:, :cols], (((0,), (0,)), ((), ())), preferred_element_type=F32
    ).astype(BF)
    mine_ref[...] = picked[:slots]
    other_ref[...] = picked[slots:]


def readout_kernel(mine_ref, got_ref, norm_ref, mem_ref, out_ref, lift, read):
    slots, kv = mem_ref.shape[0], mem_ref.shape[1]
    heads = mine_ref.shape[1] // DH
    group = heads // kv
    lifted = elu_plus(mine_ref[...].astype(F32) + got_ref[...].astype(F32))
    for h in range(heads):
        lift[:, h, :] = lifted[:, h * DH : (h + 1) * DH]
    which = lax.broadcasted_iota(jnp.int32, (heads, DH), 0) // group
    for t in range(slots):
        row = lift[t]
        norm = jnp.zeros((heads, DH), F32)
        for k in range(kv):
            norm = jnp.where(which == k, norm_ref[t, k : k + 1, :], norm)
        denom = jnp.sum(row * norm, axis=1, keepdims=True)
        high = row.astype(BF).astype(F32)
        both = jnp.concatenate([high, row - high], axis=0).astype(BF)
        numer = jnp.zeros((heads, DH), F32)
        for k in range(kv):
            mem = mem_ref[t, k]
            mem_high = mem.astype(BF)
            mem_low = (mem - mem_high.astype(F32)).astype(BF)
            parts = jnp.concatenate([mem_high, mem_low], axis=1)
            every = jnp.dot(both, parts, preferred_element_type=F32)
            one = every[:heads, :DH] + (
                every[heads:, :DH] + every[:heads, DH:] + every[heads:, DH:]
            )
            numer = jnp.where(which == k, one, numer)
        read[t] = (numer / denom).astype(BF).astype(F32)
    for h in range(heads):
        out_ref[:, h * DH : (h + 1) * DH] = read[:, h, :].astype(BF)


def spread_kernel(sel_ref, mine_ref, other_ref, *out_refs):
    reads = jnp.concatenate([mine_ref[...], other_ref[...]], axis=0)
    rows = out_refs[0].shape[0]
    every = jnp.dot(sel_ref[...], reads, preferred_element_type=F32).astype(BF)
    for i, out in enumerate(out_refs):
        out[...] = every[i * rows : (i + 1) * rows]


def fetch_kernel(*refs):
    *refs, sems = refs
    half = len(refs) // 2
    copies = []
    for a, (src, dst) in enumerate(zip(refs[:half], refs[half:])):
        count = min(sems.shape[1], src.shape[0])
        depth = src.shape[0] // count
        for i in range(count):
            at = pl.ds(i * depth, depth)
            copies.append(pltpu.make_async_copy(src.at[at], dst.at[at], sems.at[a, i]))
    for c in copies:
        c.start()
    for c in copies:
        c.wait()


def columns_of(w_ref, tp, j):
    cols = w_ref.shape[1] // tp
    first = lax.rem(lax.axis_index("tp") + j, tp) * cols
    return w_ref[:, pl.ds(pl.multiple_of(first, DH), cols)]


def away_kernel(tp, gate_hbm, kept_ref, got_ref, local_ref, w_ref, out_ref, att_ref, gate_ref, small):
    heads = local_ref.shape[1]
    for c in fetch_all([(gate_hbm, gate_ref)], small):
        c.wait()
    gate = jax.nn.sigmoid(gate_ref[...])
    for h in range(heads):
        at = slice(h * DH, (h + 1) * DH)
        memory = kept_ref[:, at].astype(F32) + got_ref[:, at].astype(F32)
        mix = gate[:, h : h + 1]
        att_ref[:, at] = (mix * memory + (1.0 - mix) * local_ref[:, h, :]).astype(BF)
    for j in range(1, tp):
        out_ref[j - 1] = jnp.dot(
            att_ref[...], columns_of(w_ref, tp, j), preferred_element_type=F32
        )


def home_kernel(tp, att_ref, w_ref, out_ref):
    out_ref[...] = jnp.dot(att_ref[...], columns_of(w_ref, tp, 0), preferred_element_type=F32)


def body(seg, tp, tokens, w_query, w_key, w_value, w_out, gate_bias, mem_store, norm_store,
         k_cache, v_cache, home_owner, home_slot, cache_len, win_start):
    rows, width = tokens.shape
    cols = w_query.shape[1]
    heads = cols // DH
    window = k_cache.shape[1]
    kv_cols = k_cache.shape[2]
    kv = kv_cols // DH
    slots = mem_store.shape[0]
    chips = seg // 2
    zs = chips // 2
    sds = jax.ShapeDtypeStruct
    dma = pltpu.SemaphoreType.DMA

    def swap(value, mask):
        return lax.ppermute(value, "seg", [(i, i ^ mask) for i in range(seg)])

    q_blocks = 16
    query, query_heads = call(
        query_kernel, "query",
        [sds((rows, cols + DH), BF), sds((rows, heads, DH), F32)],
        [HBM] * 4,
        [pltpu.SMEM((rows,), jnp.int32)] * 2
        + [pltpu.VMEM((rows, width), BF),
           pltpu.VMEM((q_blocks, width // q_blocks, cols), BF), dma((q_blocks,)), dma((3,))],
        24, 2 * rows * width * cols, 2 * width * cols,
        (home_owner, home_slot, tokens, w_query),
    )
    near = swap(query, seg // 2)
    kv_blocks = 8
    key_new, value_new = call(
        keyval_kernel, "keyval",
        [sds((rows, kv_cols), BF)] * 2,
        [ANY, ANY, ANY],
        [pltpu.VMEM((rows, width), BF)]
        + [pltpu.VMEM((kv_blocks, width // kv_blocks, kv_cols), BF)] * 2
        + [dma((2, kv_blocks)), dma((1,))],
        12, 4 * rows * width * kv_cols, 4 * width * kv_cols,
        (tokens, w_key, w_value),
    )
    near, key_new, value_new = lax.optimization_barrier((near, key_new, value_new))
    pair = jnp.concatenate([query, near], axis=0)
    far = [swap(pair, 2 * j) for j in range(1, zs)]
    probs, own_prob = call(
        probs_kernel, "probs",
        [sds((rows, heads, window), BF), sds((rows, heads, DH), F32)],
        [ANY, ANY, VM, VM, HBM],
        [pltpu.SMEM((rows,), jnp.int32)] * 2
        + [pltpu.VMEM((rows, window, kv_cols), BF), pltpu.VMEM((rows, heads, window), F32),
           pltpu.VMEM((rows, heads, kv_cols), BF), dma((rows,)), dma((2,))],
        20, 2 * rows * heads * window * kv_cols, rows * window * kv_cols,
        (cache_len, win_start, query_heads, key_new, k_cache),
    )
    far, probs, own_prob = lax.optimization_barrier((far, probs, own_prob))
    mine, other, sel = call(
        functools.partial(route_kernel, cols, slots), "route",
        [sds((slots, cols), BF)] * 2 + [sds((chips * rows, 2 * slots), BF)],
        [VM] * zs, [], 8, 4 * slots * chips * rows * cols, 0,
        (pair, *far),
    )
    got = swap(other, 1)
    mem_fast, norm_fast = call(
        fetch_kernel, "fetch_memory",
        [sds(mem_store.shape, F32), sds(norm_store.shape, F32)],
        [ANY, ANY], [dma((2, 8))],
        4, 0, 4 * slots * kv * DH * DH,
        (mem_store, norm_store),
    )
    got, mem_fast, norm_fast = lax.optimization_barrier((got, mem_fast, norm_fast))
    read = call(
        readout_kernel, "readout",
        sds((slots, cols), BF), [VM] * 4, [pltpu.VMEM((slots, heads, DH), F32)] * 2,
        8, 8 * slots * heads * DH * DH, 0,
        (mine, got, norm_fast, mem_fast),
    )
    partner = swap(read, 1)
    here, *away = call(
        spread_kernel, "spread",
        [sds((2 * rows, cols), BF)] * zs,
        [VM] * 3, [], 8, 4 * slots * chips * rows * cols, 0,
        (sel, read, partner),
    )
    back = [swap(away[j - 1], 2 * j) for j in range(1, zs)]
    away, probs = lax.optimization_barrier((away, probs))
    local_read = call(
        values_kernel, "values",
        sds((rows, heads, DH), F32),
        [ANY, ANY, VM, VM, VM, HBM],
        [pltpu.SMEM((rows,), jnp.int32)] * 2
        + [pltpu.VMEM((rows, window, kv_cols), BF), dma((rows,)), dma((2,))],
        18, 2 * rows * heads * window * kv_cols, rows * window * kv_cols,
        (cache_len, win_start, probs, own_prob, value_new.reshape(rows, 1, kv_cols), v_cache),
    )
    back, local_read = lax.optimization_barrier((back, local_read))
    for value in back:
        here = here + value
    kept, leaving = here[:rows], here[rows:]
    last = swap(leaving, seg // 2)
    w_fast = call(
        fetch_kernel, "fetch",
        [sds(w_out.shape, BF)], [ANY], [dma((1, 16))],
        4, 0, 2 * w_out.shape[0] * w_out.shape[1],
        (w_out,),
    )[0]
    last, w_fast = lax.optimization_barrier((last, w_fast))
    out_cols = w_out.shape[1] // tp
    others, attended = call(
        functools.partial(away_kernel, tp), "away",
        [sds((tp - 1, rows, out_cols), F32), sds((rows, cols), BF)],
        [ANY, VM, VM, VM, VM], [pltpu.VMEM((1, heads), F32), dma((1,))],
        4, 2 * rows * cols * (w_out.shape[1] - out_cols), 0,
        (gate_bias.reshape(1, heads), kept, last, local_read, w_fast),
    )
    came = [
        lax.ppermute(others[j - 1], "tp", [(i, (i + j) % tp) for i in range(tp)])
        for j in range(1, tp)
    ]
    result = call(
        functools.partial(home_kernel, tp), "home",
        sds((rows, out_cols), F32), [VM, VM], [],
        4, 2 * rows * cols * out_cols, 0,
        (attended, w_fast),
    )
    came, result = lax.optimization_barrier((came, result))
    for value in came:
        result = result + value
    return result.astype(BF)


def solution(mesh):
    placed = (
        P("seg", None),
        P(None, "tp"),
        P(None, "tp"),
        P(None, "tp"),
        P("tp", None),
        P("tp"),
        P("seg", "tp", None, None),
        P("seg", "tp", None),
        P("seg", None, "tp"),
        P("seg", None, "tp"),
        P("seg"),
        P("seg"),
        P("seg"),
        P("seg"),
    )
    inner = functools.partial(body, mesh.shape["seg"], mesh.shape["tp"])
    return jax.shard_map(
        inner, mesh=mesh, in_specs=placed, out_specs=P("seg", "tp"), check_vma=False
    )
```

```python
import functools

import jax
import jax.numpy as jnp
from jax import lax
from jax.experimental import pallas as pl
from jax.experimental.pallas import tpu as pltpu
from jax.sharding import PartitionSpec as P

DH = 128
MIB = 2**20
STRETCHES = 8
BF = jnp.bfloat16
F32 = jnp.float32

ANY = pl.BlockSpec(memory_space=pl.ANY)
VM = pl.BlockSpec(memory_space=pltpu.VMEM)
HBM = pl.BlockSpec(memory_space=pltpu.HBM)


def call(kernel, name, out_shape, in_specs, scratch, mib, flops, nbytes, args):
    many = isinstance(out_shape, (list, tuple))
    args = [
        pltpu.with_memory_space_constraint(a, pltpu.HBM) if spec is HBM else a
        for a, spec in zip(args, in_specs)
    ]
    return pl.pallas_call(
        kernel,
        name=name,
        out_shape=out_shape,
        in_specs=in_specs,
        out_specs=[VM] * len(out_shape) if many else VM,
        scratch_shapes=scratch,
        compiler_params=pltpu.CompilerParams(vmem_limit_bytes=mib * MIB),
        cost_estimate=pl.CostEstimate(flops=flops, bytes_accessed=nbytes, transcendentals=0),
    )(*args)


def elu_plus(values):
    return jnp.where(values > 0, values + 1.0, jnp.exp(jnp.minimum(values, 0.0)))


def fetch_all(pairs, sems):
    copies = [pltpu.make_async_copy(a, b, sems.at[i]) for i, (a, b) in enumerate(pairs)]
    for c in copies:
        c.start()
    return copies


def query_kernel(owner_hbm, slot_hbm, owner2_hbm, slot2_hbm, x_hbm, x2_hbm, w_ref, q_ref, give_ref,
                 owner_ref, slot_ref, owner2_ref, slot2_ref, x_ref, buf, sems, small):
    rows = x_hbm.shape[0]
    count, depth, cols = buf.shape
    first = pl.multiple_of(lax.rem(lax.axis_index("seg"), 2) * cols, DH)

    def copy(i):
        at = pl.ds(i * depth, depth)
        return pltpu.make_async_copy(w_ref.at[at, pl.ds(first, cols)], buf.at[i], sems.at[i])

    ready = fetch_all(
        [(x_hbm, x_ref.at[:rows]), (x2_hbm, x_ref.at[rows:]), (owner_hbm, owner_ref),
         (slot_hbm, slot_ref), (owner2_hbm, owner2_ref), (slot2_hbm, slot2_ref)],
        small,
    )
    for i in range(count):
        copy(i).start()
    for c in ready:
        c.wait()
    row = lax.broadcasted_iota(jnp.int32, (2 * rows, DH), 0)
    lane = lax.broadcasted_iota(jnp.int32, (2 * rows, DH), 1)
    extra = jnp.zeros((2 * rows, DH), F32)
    for r in range(rows):
        for at, one, two in ((r, owner_ref, slot_ref), (rows + r, owner2_ref, slot2_ref)):
            extra = jnp.where((row == at) & (lane == 0), one[r].astype(F32), extra)
            extra = jnp.where((row == at) & (lane == 1), two[r].astype(F32), extra)
    q_ref[:, cols:] = extra.astype(BF)
    total = jnp.zeros((2 * rows, cols), F32)
    for i in range(count):
        copy(i).wait()
        total = total + jnp.dot(
            x_ref[:, i * depth : (i + 1) * depth], buf[i], preferred_element_type=F32
        )
    q_ref[:, :cols] = total.astype(BF)
    give_ref[...] = total[rows:].astype(BF)


def both_halves(own, got):
    even = lax.rem(lax.axis_index("seg"), 2) == 0
    return jnp.where(even, own, got), jnp.where(even, got, own)


def keyval_kernel(x_hbm, wk_ref, wv_ref, k_ref, v_ref, x_ref, bufk, bufv, sems, small):
    count, depth = bufk.shape[0], bufk.shape[1]

    def copies(i):
        at = pl.ds(i * depth, depth)
        return (
            pltpu.make_async_copy(wk_ref.at[at, :], bufk.at[i], sems.at[0, i]),
            pltpu.make_async_copy(wv_ref.at[at, :], bufv.at[i], sems.at[1, i]),
        )

    first = fetch_all([(x_hbm, x_ref)], small)
    for i in range(count):
        for c in copies(i):
            c.start()
    first[0].wait()
    key = jnp.zeros(k_ref.shape, F32)
    val = jnp.zeros(v_ref.shape, F32)
    for i in range(count):
        for c in copies(i):
            c.wait()
        part = x_ref[:, i * depth : (i + 1) * depth]
        key = key + jnp.dot(part, bufk[i], preferred_element_type=F32)
        val = val + jnp.dot(part, bufv[i], preferred_element_type=F32)
    k_ref[...] = key.astype(BF)
    v_ref[...] = val.astype(BF)


def live_blocks(start_ref, len_ref, r):
    lo = start_ref[r] // DH
    return lo, jnp.maximum((len_ref[r] + DH - 1) // DH - lo, 0)


def each_copy(cache_ref, buf, sems, r, lo, count, act):
    size = 1
    while size < buf.shape[1] // DH:
        size *= 2
    while size:
        here, now = lo, size

        @pl.when((count & now) != 0)
        def _():
            at = pl.ds(pl.multiple_of(here * DH, DH), now * DH)
            act(pltpu.make_async_copy(cache_ref.at[r, at, :], buf.at[r, at, :], sems.at[r]))

        lo = lo + (count & size)
        size //= 2


def by_length(window, lo, count, step, act):
    need = (count * DH + step - 1) // step
    for n in range(1, window // step + 1):
        first = pl.multiple_of(jnp.minimum(lo * DH, window - n * step), DH)
        pl.when(need == n)(functools.partial(act, first, n * step))


def scores_kernel(len_hbm, start_hbm, own_ref, got_ref, kc_ref, score_ref, qh_ref, len_ref, start_ref,
                  buf, wide_ref, sems, small):
    rows, heads, window = score_ref.shape
    kv = kc_ref.shape[2] // DH
    group = heads // kv
    for c in fetch_all([(len_hbm, len_ref), (start_hbm, start_ref)], small):
        c.wait()

    @pl.loop(0, rows)
    def _(r):
        lo, count = live_blocks(start_ref, len_ref, r)
        each_copy(kc_ref, buf, sems, r, lo, count, lambda c: c.start())

    cols = got_ref.shape[1]
    halves = both_halves(own_ref[:rows, :cols].astype(F32), got_ref[...].astype(F32))
    for h in range(heads):
        at = (h * DH) % cols
        qh_ref[:, h, :] = halves[h * DH // cols][:, at : at + DH]
    which = lax.broadcasted_iota(jnp.int32, (heads, DH), 0) // group
    for r in range(rows):
        q = qh_ref[r]
        for k in range(kv):
            wide_ref[r, :, k * DH : (k + 1) * DH] = jnp.where(which == k, q, 0.0).astype(BF)

    @pl.loop(0, rows)
    def _(r):
        lo, count = live_blocks(start_ref, len_ref, r)
        each_copy(kc_ref, buf, sems, r, lo, count, lambda c: c.wait())

        def product(first, size):
            at = pl.ds(first, size)
            score_ref[r, :, at] = lax.dot_general(
                wide_ref[r], buf[r, at, :], (((1,), (1,)), ((), ())), preferred_element_type=F32
            )

        by_length(window, lo, count, window // STRETCHES, product)


def probs_kernel(len_hbm, start_hbm, qh_ref, kn_ref, score_ref, p_ref, own_ref, len_ref, start_ref,
                 small):
    rows, heads, window = p_ref.shape
    kv = kn_ref.shape[1] // DH
    group = heads // kv
    copies = fetch_all([(len_hbm, len_ref), (start_hbm, start_ref)], small)
    which = lax.broadcasted_iota(jnp.int32, (heads, DH), 0) // group
    position = lax.broadcasted_iota(jnp.int32, (heads, window), 1)
    scale = DH ** (-0.5)
    for c in copies:
        c.wait()
    for r in range(rows):
        q = qh_ref[r]
        key = jnp.zeros((heads, DH), F32)
        for k in range(kv):
            one = kn_ref[r : r + 1, k * DH : (k + 1) * DH].astype(F32)
            key = jnp.where(which == k, one, key)
        own = jnp.sum(q * key, axis=1, keepdims=True) * scale
        live = (position >= start_ref[r]) & (position < len_ref[r])
        s = jnp.where(live, score_ref[r] * scale, -jnp.inf)
        top = jnp.maximum(jnp.max(s, axis=1, keepdims=True), own)
        weight = jnp.exp(s - top)
        own_weight = jnp.exp(own - top)
        inverse = 1.0 / (jnp.sum(weight, axis=1, keepdims=True) + own_weight)
        p_ref[r] = (weight * inverse).astype(BF)
        prob = (own_weight * inverse).astype(BF).astype(F32)
        own_ref[r] = jnp.broadcast_to(prob, (heads, DH))


def values_kernel(len_hbm, start_hbm, p_ref, own_ref, vn_ref, vc_ref, out_ref, len_ref, start_ref,
                  buf, sems, small):
    rows, heads, window = p_ref.shape
    kv = vc_ref.shape[2] // DH
    group = heads // kv
    for c in fetch_all([(len_hbm, len_ref), (start_hbm, start_ref)], small):
        c.wait()

    @pl.loop(0, rows)
    def _(r):
        lo, count = live_blocks(start_ref, len_ref, r)
        each_copy(vc_ref, buf, sems, r, lo, count, lambda c: c.start())

    which = lax.broadcasted_iota(jnp.int32, (heads, DH), 0) // group
    nothing = jnp.zeros((DH, kv * DH), BF)

    @pl.loop(0, rows)
    def _(r):
        lo, count = live_blocks(start_ref, len_ref, r)
        base = jnp.zeros((heads, DH), F32)
        for k in range(kv):
            value = vn_ref[r, :, k * DH : (k + 1) * DH].astype(F32)
            base = jnp.where(which == k, own_ref[r] * value, base)
        out_ref[r] = base

        def clear(b):
            buf[r, pl.ds(pl.multiple_of(b * DH, DH), DH), :] = nothing

        def product(first, size):
            pl.loop(first // DH, lo)(clear)
            pl.loop(lo + count, (first + size) // DH)(clear)
            each_copy(vc_ref, buf, sems, r, lo, count, lambda c: c.wait())
            at = pl.ds(first, size)
            every = jnp.dot(p_ref[r, :, at], buf[r, at, :], preferred_element_type=F32)
            read = jnp.zeros((heads, DH), F32)
            for k in range(kv):
                read = jnp.where(which == k, every[:, k * DH : (k + 1) * DH], read)
            out_ref[r] += read

        by_length(window, lo, count, window // STRETCHES, product)


def route_kernel(own_rows, cols, slots, *refs):
    *row_refs, mine_ref, other_ref, sel_ref = refs
    me = lax.axis_index("seg")
    half = lax.rem(me, 2)
    first = me - half
    rows = jnp.concatenate([r[...] for r in row_refs], axis=0)
    owner = rows[:, cols : cols + 1].astype(F32).astype(jnp.int32)
    slot = rows[:, cols + 1 : cols + 2].astype(F32).astype(jnp.int32)
    rel = owner - first
    near = (rel >= 0) & (rel < 2)
    target = jnp.where(rel == half, 0, slots) + slot
    target = jnp.where(near, target, -1)
    lane = lax.broadcasted_iota(jnp.int32, (rows.shape[0], 2 * slots), 1)
    sel = (lane == target).astype(F32)
    step = own_rows
    sel_ref[...] = jnp.concatenate(
        [sel[i : i + step] for i in range(0, rows.shape[0], 2 * step)], axis=0
    ).astype(BF)
    sel = sel.astype(BF)
    picked = lax.dot_general(
        sel, rows[:, :cols], (((0,), (0,)), ((), ())), preferred_element_type=F32
    ).astype(BF)
    mine_ref[...] = picked[:slots]
    other_ref[...] = picked[slots:]


def readout_kernel(mine_ref, got_ref, norm_ref, mem_ref, out_ref, lift, read):
    slots, kv = mem_ref.shape[0], mem_ref.shape[1]
    cols = mine_ref.shape[1]
    heads = 2 * cols // DH
    group = heads // kv
    halves = both_halves(
        elu_plus(mine_ref[...].astype(F32)), elu_plus(got_ref[...].astype(F32))
    )
    for h in range(heads):
        at = (h * DH) % cols
        lift[:, h, :] = halves[h * DH // cols][:, at : at + DH]
    which = lax.broadcasted_iota(jnp.int32, (heads, DH), 0) // group
    for t in range(slots):
        row = lift[t]
        norm = jnp.zeros((heads, DH), F32)
        for k in range(kv):
            norm = jnp.where(which == k, norm_ref[t, k : k + 1, :], norm)
        denom = jnp.sum(row * norm, axis=1, keepdims=True)
        high = row.astype(BF).astype(F32)
        both = jnp.concatenate([high, row - high], axis=0).astype(BF)
        numer = jnp.zeros((heads, DH), F32)
        for k in range(kv):
            mem = mem_ref[t, k]
            mem_high = mem.astype(BF)
            mem_low = (mem - mem_high.astype(F32)).astype(BF)
            parts = jnp.concatenate([mem_high, mem_low], axis=1)
            every = jnp.dot(both, parts, preferred_element_type=F32)
            one = every[:heads, :DH] + (
                every[heads:, :DH] + every[:heads, DH:] + every[heads:, DH:]
            )
            numer = jnp.where(which == k, one, numer)
        read[t] = (numer / denom).astype(BF).astype(F32)
    for h in range(heads):
        out_ref[:, h * DH : (h + 1) * DH] = read[:, h, :].astype(BF)


def spread_kernel(sel_ref, mine_ref, other_ref, *out_refs):
    reads = jnp.concatenate([mine_ref[...], other_ref[...]], axis=0)
    rows = out_refs[0].shape[0]
    every = jnp.dot(sel_ref[...], reads, preferred_element_type=F32).astype(BF)
    for i, out in enumerate(out_refs):
        out[...] = every[i * rows : (i + 1) * rows]


def fetch_kernel(*refs):
    *refs, sems = refs
    half = len(refs) // 2
    copies = []
    for a, (src, dst) in enumerate(zip(refs[:half], refs[half:])):
        count = min(sems.shape[1], src.shape[0])
        depth = src.shape[0] // count
        for i in range(count):
            at = pl.ds(i * depth, depth)
            copies.append(pltpu.make_async_copy(src.at[at], dst.at[at], sems.at[a, i]))
    for c in copies:
        c.start()
    for c in copies:
        c.wait()


def columns_of(w_ref, tp, j):
    cols = w_ref.shape[1] // tp
    first = lax.rem(lax.axis_index("tp") + j, tp) * cols
    return w_ref[:, pl.ds(pl.multiple_of(first, DH), cols)]


def away_kernel(tp, gate_hbm, kept_ref, got_ref, local_ref, w_ref, out_ref, att_ref, gate_ref, small):
    heads = local_ref.shape[1]
    for c in fetch_all([(gate_hbm, gate_ref)], small):
        c.wait()
    gate = jax.nn.sigmoid(gate_ref[...])
    for h in range(heads):
        at = slice(h * DH, (h + 1) * DH)
        memory = kept_ref[:, at].astype(F32) + got_ref[:, at].astype(F32)
        mix = gate[:, h : h + 1]
        att_ref[:, at] = (mix * memory + (1.0 - mix) * local_ref[:, h, :]).astype(BF)
    for j in range(1, tp):
        out_ref[j - 1] = jnp.dot(
            att_ref[...], columns_of(w_ref, tp, j), preferred_element_type=F32
        ).astype(out_ref.dtype)


def home_kernel(tp, att_ref, w_ref, out_ref):
    out_ref[...] = jnp.dot(att_ref[...], columns_of(w_ref, tp, 0), preferred_element_type=F32)


def body(seg, tp, tokens, w_query, w_key, w_value, w_out, gate_bias, mem_store, norm_store,
         k_cache, v_cache, home_owner, home_slot, cache_len, win_start):
    rows, width = tokens.shape
    cols = w_query.shape[1]
    heads = cols // DH
    window = k_cache.shape[1]
    kv_cols = k_cache.shape[2]
    kv = kv_cols // DH
    slots = mem_store.shape[0]
    chips = seg // 2
    zs = chips // 2
    sds = jax.ShapeDtypeStruct
    dma = pltpu.SemaphoreType.DMA

    def swap(value, mask):
        return lax.ppermute(value, "seg", [(i, i ^ mask) for i in range(seg)])

    q_blocks = 16
    half = cols // 2
    query, give = call(
        query_kernel, "query",
        [sds((2 * rows, half + DH), BF), sds((rows, half), BF)],
        [HBM, HBM, ANY, ANY, HBM, ANY, HBM],
        [pltpu.SMEM((rows,), jnp.int32)] * 4
        + [pltpu.VMEM((2 * rows, width), BF),
           pltpu.VMEM((q_blocks, width // q_blocks, half), BF), dma((q_blocks,)), dma((6,))],
        16, 4 * rows * width * half, 2 * width * half,
        (home_owner, home_slot, swap(home_owner, 1), swap(home_slot, 1), tokens, swap(tokens, 1),
         w_query),
    )
    query, give, tokens_late = lax.optimization_barrier((query, give, tokens))
    near = swap(query, seg // 2)
    query_got = swap(give, 1)
    kv_blocks = 8
    key_new, value_new = call(
        keyval_kernel, "keyval",
        [sds((rows, kv_cols), BF)] * 2,
        [ANY, ANY, ANY],
        [pltpu.VMEM((rows, width), BF)]
        + [pltpu.VMEM((kv_blocks, width // kv_blocks, kv_cols), BF)] * 2
        + [dma((2, kv_blocks)), dma((1,))],
        12, 4 * rows * width * kv_cols, 4 * width * kv_cols,
        (tokens_late, w_key, w_value),
    )
    near, query_got, key_new, value_new = lax.optimization_barrier(
        (near, query_got, key_new, value_new)
    )
    pair = jnp.concatenate([query, near], axis=0)
    far = [swap(pair, 2 * j) for j in range(1, zs)]
    scores, query_heads = call(
        scores_kernel, "scores",
        [sds((rows, heads, window), F32), sds((rows, heads, DH), F32)],
        [ANY, ANY, VM, VM, HBM],
        [pltpu.SMEM((rows,), jnp.int32)] * 2
        + [pltpu.VMEM((rows, window, kv_cols), BF), pltpu.VMEM((rows, heads, kv_cols), BF),
           dma((rows,)), dma((2,))],
        20, 2 * rows * heads * window * kv_cols, rows * window * kv_cols,
        (cache_len, win_start, query, query_got, k_cache),
    )
    far, scores, query_heads = lax.optimization_barrier((far, scores, query_heads))
    mine, other, sel = call(
        functools.partial(route_kernel, rows, half, slots), "route",
        [sds((slots, half), BF)] * 2 + [sds((chips * rows, 2 * slots), BF)],
        [VM] * zs, [], 8, 4 * slots * chips * rows * cols, 0,
        (pair, *far),
    )
    got = swap(other, 1)
    mem_fast, norm_fast = call(
        fetch_kernel, "fetch_memory",
        [sds(mem_store.shape, F32), sds(norm_store.shape, F32)],
        [ANY, ANY], [dma((2, 8))],
        4, 0, 4 * slots * kv * DH * DH,
        (mem_store, norm_store),
    )
    got, mem_fast, norm_fast = lax.optimization_barrier((got, mem_fast, norm_fast))
    read = call(
        readout_kernel, "readout",
        sds((slots, cols), BF), [VM] * 4, [pltpu.VMEM((slots, heads, DH), F32)] * 2,
        8, 8 * slots * heads * DH * DH, 0,
        (mine, got, norm_fast, mem_fast),
    )
    partner = swap(read, 1)
    probs, own_prob = call(
        probs_kernel, "probs",
        [sds((rows, heads, window), BF), sds((rows, heads, DH), F32)],
        [ANY, ANY, VM, VM, VM],
        [pltpu.SMEM((rows,), jnp.int32)] * 2 + [dma((2,))],
        8, 20 * rows * heads * window, 0,
        (cache_len, win_start, query_heads, key_new, scores),
    )
    partner, probs, own_prob = lax.optimization_barrier((partner, probs, own_prob))
    here, *away = call(
        spread_kernel, "spread",
        [sds((2 * rows, cols), BF)] * zs,
        [VM] * 3, [], 8, 4 * slots * chips * rows * cols, 0,
        (sel, read, partner),
    )
    back = [swap(away[j - 1], 2 * j) for j in range(1, zs)]
    away, probs = lax.optimization_barrier((away, probs))
    local_read = call(
        values_kernel, "values",
        sds((rows, heads, DH), F32),
        [ANY, ANY, VM, VM, VM, HBM],
        [pltpu.SMEM((rows,), jnp.int32)] * 2
        + [pltpu.VMEM((rows, window, kv_cols), BF), dma((rows,)), dma((2,))],
        18, 2 * rows * heads * window * kv_cols, rows * window * kv_cols,
        (cache_len, win_start, probs, own_prob, value_new.reshape(rows, 1, kv_cols), v_cache),
    )
    back, local_read = lax.optimization_barrier((back, local_read))
    for value in back:
        here = here + value
    kept, leaving = here[:rows], here[rows:]
    last = swap(leaving, seg // 2)
    w_fast = call(
        fetch_kernel, "fetch",
        [sds(w_out.shape, BF)], [ANY], [dma((1, 16))],
        4, 0, 2 * w_out.shape[0] * w_out.shape[1],
        (w_out,),
    )[0]
    last, w_fast = lax.optimization_barrier((last, w_fast))
    out_cols = w_out.shape[1] // tp
    others, attended = call(
        functools.partial(away_kernel, tp), "away",
        [sds((tp - 1, rows, out_cols), F32), sds((rows, cols), BF)],
        [ANY, VM, VM, VM, VM], [pltpu.VMEM((1, heads), F32), dma((1,))],
        4, 2 * rows * cols * (w_out.shape[1] - out_cols), 0,
        (gate_bias.reshape(1, heads), kept, last, local_read, w_fast),
    )
    came = [
        lax.ppermute(others[j - 1], "tp", [(i, (i + j) % tp) for i in range(tp)])
        for j in range(1, tp)
    ]
    result = call(
        functools.partial(home_kernel, tp), "home",
        sds((rows, out_cols), F32), [VM, VM], [],
        4, 2 * rows * cols * out_cols, 0,
        (attended, w_fast),
    )
    came, result = lax.optimization_barrier((came, result))
    for value in came:
        result = result + value
    return result.astype(BF)


def solution(mesh):
    placed = (
        P("seg", None),
        P(None, "tp"),
        P(None, "tp"),
        P(None, "tp"),
        P("tp", None),
        P("tp"),
        P("seg", "tp", None, None),
        P("seg", "tp", None),
        P("seg", None, "tp"),
        P("seg", None, "tp"),
        P("seg"),
        P("seg"),
        P("seg"),
        P("seg"),
    )
    inner = functools.partial(body, mesh.shape["seg"], mesh.shape["tp"])
    return jax.shard_map(
        inner, mesh=mesh, in_specs=placed, out_specs=P("seg", "tp"), check_vma=False
    )
```

```python
import functools

import jax
import jax.numpy as jnp
from jax import lax
from jax.experimental import pallas as pl
from jax.experimental.pallas import tpu as pltpu
from jax.sharding import PartitionSpec as P

DH = 128
MIB = 2**20
STRETCHES = 8
BF = jnp.bfloat16
F32 = jnp.float32

ANY = pl.BlockSpec(memory_space=pl.ANY)
VM = pl.BlockSpec(memory_space=pltpu.VMEM)
HBM = pl.BlockSpec(memory_space=pltpu.HBM)


def call(kernel, name, out_shape, in_specs, scratch, mib, flops, nbytes, args):
    many = isinstance(out_shape, (list, tuple))
    args = [
        pltpu.with_memory_space_constraint(a, pltpu.HBM) if spec is HBM else a
        for a, spec in zip(args, in_specs)
    ]
    return pl.pallas_call(
        kernel,
        name=name,
        out_shape=out_shape,
        in_specs=in_specs,
        out_specs=[VM] * len(out_shape) if many else VM,
        scratch_shapes=scratch,
        compiler_params=pltpu.CompilerParams(vmem_limit_bytes=mib * MIB),
        cost_estimate=pl.CostEstimate(flops=flops, bytes_accessed=nbytes, transcendentals=0),
    )(*args)


def elu_plus(values):
    return jnp.where(values > 0, values + 1.0, jnp.exp(jnp.minimum(values, 0.0)))


def fetch_all(pairs, sems):
    copies = [pltpu.make_async_copy(a, b, sems.at[i]) for i, (a, b) in enumerate(pairs)]
    for c in copies:
        c.start()
    return copies


def query_kernel(owner_hbm, slot_hbm, owner2_hbm, slot2_hbm, len_hbm, start_hbm, x_hbm, x2_hbm, w_ref,
                 q_ref, give_ref, limit_ref, owner_ref, slot_ref, owner2_ref, slot2_ref, len_ref,
                 start_ref, x_ref, buf, sems, small):
    rows = x_hbm.shape[0]
    count, depth, cols = buf.shape
    first = pl.multiple_of(lax.rem(lax.axis_index("seg"), 2) * cols, DH)

    def copy(i):
        at = pl.ds(i * depth, depth)
        return pltpu.make_async_copy(w_ref.at[at, pl.ds(first, cols)], buf.at[i], sems.at[i])

    ready = fetch_all(
        [(x_hbm, x_ref.at[:rows]), (x2_hbm, x_ref.at[rows:]), (owner_hbm, owner_ref),
         (slot_hbm, slot_ref), (owner2_hbm, owner2_ref), (slot2_hbm, slot2_ref),
         (len_hbm, len_ref), (start_hbm, start_ref)],
        small,
    )
    for i in range(count):
        copy(i).start()
    for c in ready:
        c.wait()
    row = lax.broadcasted_iota(jnp.int32, (2 * rows, DH), 0)
    lane = lax.broadcasted_iota(jnp.int32, (2 * rows, DH), 1)
    extra = jnp.zeros((2 * rows, DH), F32)
    for r in range(rows):
        for at, one, two in ((r, owner_ref, slot_ref), (rows + r, owner2_ref, slot2_ref)):
            extra = jnp.where((row == at) & (lane == 0), one[r].astype(F32), extra)
            extra = jnp.where((row == at) & (lane == 1), two[r].astype(F32), extra)
    q_ref[:, cols:] = extra.astype(BF)
    row = lax.broadcasted_iota(jnp.int32, limit_ref.shape, 0)
    lane = lax.broadcasted_iota(jnp.int32, limit_ref.shape, 1)
    limit = jnp.zeros(limit_ref.shape, F32)
    for r in range(rows):
        ends = jnp.where(row == 0, len_ref[r].astype(F32), start_ref[r].astype(F32))
        limit = jnp.where(lane == r, ends, limit)
    limit_ref[...] = limit
    total = jnp.zeros((2 * rows, cols), F32)
    for i in range(count):
        copy(i).wait()
        total = total + jnp.dot(
            x_ref[:, i * depth : (i + 1) * depth], buf[i], preferred_element_type=F32
        )
    q_ref[:, :cols] = total.astype(BF)
    give_ref[...] = total[rows:].astype(BF)


def read_limits(limit_ref, len_ref, start_ref):
    shape = (1, limit_ref.shape[1])
    lane = lax.broadcasted_iota(jnp.int32, shape, 1)
    for r in range(len_ref.shape[0]):
        for i, out in enumerate((len_ref, start_ref)):
            one = jnp.where(lane == r, limit_ref[i : i + 1, :], 0.0)
            out[r] = jnp.sum(one).astype(jnp.int32)


def both_halves(own, got):
    even = lax.rem(lax.axis_index("seg"), 2) == 0
    return jnp.where(even, own, got), jnp.where(even, got, own)


def keyval_kernel(x_hbm, wk_ref, wv_ref, k_ref, v_ref, x_ref, bufk, bufv, sems, small):
    count, depth = bufk.shape[0], bufk.shape[1]

    def copies(i):
        at = pl.ds(i * depth, depth)
        return (
            pltpu.make_async_copy(wk_ref.at[at, :], bufk.at[i], sems.at[0, i]),
            pltpu.make_async_copy(wv_ref.at[at, :], bufv.at[i], sems.at[1, i]),
        )

    first = fetch_all([(x_hbm, x_ref)], small)
    for i in range(count):
        for c in copies(i):
            c.start()
    first[0].wait()
    key = jnp.zeros(k_ref.shape, F32)
    val = jnp.zeros(v_ref.shape, F32)
    for i in range(count):
        for c in copies(i):
            c.wait()
        part = x_ref[:, i * depth : (i + 1) * depth]
        key = key + jnp.dot(part, bufk[i], preferred_element_type=F32)
        val = val + jnp.dot(part, bufv[i], preferred_element_type=F32)
    k_ref[...] = key.astype(BF)
    v_ref[...] = val.astype(BF)


def live_blocks(start_ref, len_ref, r):
    lo = start_ref[r] // DH
    return lo, jnp.maximum((len_ref[r] + DH - 1) // DH - lo, 0)


def each_copy(cache_ref, buf, sems, r, lo, count, act):
    size = 1
    while size < buf.shape[1] // DH:
        size *= 2
    while size:
        here, now = lo, size

        @pl.when((count & now) != 0)
        def _():
            at = pl.ds(pl.multiple_of(here * DH, DH), now * DH)
            act(pltpu.make_async_copy(cache_ref.at[r, at, :], buf.at[r, at, :], sems.at[r]))

        lo = lo + (count & size)
        size //= 2


def by_length(window, lo, count, step, act):
    need = (count * DH + step - 1) // step
    for n in range(1, window // step + 1):
        first = pl.multiple_of(jnp.minimum(lo * DH, window - n * step), DH)
        pl.when(need == n)(functools.partial(act, first, n * step))


def scores_kernel(limit_ref, own_ref, got_ref, kc_ref, score_ref, qh_ref, len_ref, start_ref,
                  buf, wide_ref, sems):
    rows, heads, window = score_ref.shape
    kv = kc_ref.shape[2] // DH
    group = heads // kv
    read_limits(limit_ref, len_ref, start_ref)

    @pl.loop(0, rows)
    def _(r):
        lo, count = live_blocks(start_ref, len_ref, r)
        each_copy(kc_ref, buf, sems, r, lo, count, lambda c: c.start())

    cols = got_ref.shape[1]
    halves = both_halves(own_ref[:rows, :cols].astype(F32), got_ref[...].astype(F32))
    for h in range(heads):
        at = (h * DH) % cols
        qh_ref[:, h, :] = halves[h * DH // cols][:, at : at + DH]
    which = lax.broadcasted_iota(jnp.int32, (heads, DH), 0) // group
    for r in range(rows):
        q = qh_ref[r]
        for k in range(kv):
            wide_ref[r, :, k * DH : (k + 1) * DH] = jnp.where(which == k, q, 0.0).astype(BF)

    @pl.loop(0, rows)
    def _(r):
        lo, count = live_blocks(start_ref, len_ref, r)
        each_copy(kc_ref, buf, sems, r, lo, count, lambda c: c.wait())

        def product(first, size):
            at = pl.ds(first, size)
            score_ref[r, :, at] = lax.dot_general(
                wide_ref[r], buf[r, at, :], (((1,), (1,)), ((), ())), preferred_element_type=F32
            )

        by_length(window, lo, count, window // STRETCHES, product)


def probs_kernel(limit_ref, qh_ref, kn_ref, score_ref, p_ref, own_ref, len_ref, start_ref):
    rows, heads, window = p_ref.shape
    kv = kn_ref.shape[1] // DH
    group = heads // kv
    read_limits(limit_ref, len_ref, start_ref)
    which = lax.broadcasted_iota(jnp.int32, (heads, DH), 0) // group
    position = lax.broadcasted_iota(jnp.int32, (heads, window), 1)
    scale = DH ** (-0.5)
    for r in range(rows):
        q = qh_ref[r]
        key = jnp.zeros((heads, DH), F32)
        for k in range(kv):
            one = kn_ref[r : r + 1, k * DH : (k + 1) * DH].astype(F32)
            key = jnp.where(which == k, one, key)
        own = jnp.sum(q * key, axis=1, keepdims=True) * scale
        live = (position >= start_ref[r]) & (position < len_ref[r])
        s = jnp.where(live, score_ref[r] * scale, -jnp.inf)
        top = jnp.maximum(jnp.max(s, axis=1, keepdims=True), own)
        weight = jnp.exp(s - top)
        own_weight = jnp.exp(own - top)
        inverse = 1.0 / (jnp.sum(weight, axis=1, keepdims=True) + own_weight)
        p_ref[r] = (weight * inverse).astype(BF)
        prob = (own_weight * inverse).astype(BF).astype(F32)
        own_ref[r] = jnp.broadcast_to(prob, (heads, DH))


def values_kernel(limit_ref, p_ref, own_ref, vn_ref, vc_ref, out_ref, len_ref, start_ref,
                  buf, sems):
    rows, heads, window = p_ref.shape
    kv = vc_ref.shape[2] // DH
    group = heads // kv
    read_limits(limit_ref, len_ref, start_ref)

    @pl.loop(0, rows)
    def _(r):
        lo, count = live_blocks(start_ref, len_ref, r)
        each_copy(vc_ref, buf, sems, r, lo, count, lambda c: c.start())

    which = lax.broadcasted_iota(jnp.int32, (heads, DH), 0) // group
    nothing = jnp.zeros((DH, kv * DH), BF)

    @pl.loop(0, rows)
    def _(r):
        lo, count = live_blocks(start_ref, len_ref, r)
        base = jnp.zeros((heads, DH), F32)
        for k in range(kv):
            value = vn_ref[r, :, k * DH : (k + 1) * DH].astype(F32)
            base = jnp.where(which == k, own_ref[r] * value, base)
        out_ref[r] = base

        def clear(b):
            buf[r, pl.ds(pl.multiple_of(b * DH, DH), DH), :] = nothing

        def product(first, size):
            pl.loop(first // DH, lo)(clear)
            pl.loop(lo + count, (first + size) // DH)(clear)
            each_copy(vc_ref, buf, sems, r, lo, count, lambda c: c.wait())
            at = pl.ds(first, size)
            every = jnp.dot(p_ref[r, :, at], buf[r, at, :], preferred_element_type=F32)
            read = jnp.zeros((heads, DH), F32)
            for k in range(kv):
                read = jnp.where(which == k, every[:, k * DH : (k + 1) * DH], read)
            out_ref[r] += read

        by_length(window, lo, count, window // STRETCHES, product)


def route_kernel(own_rows, cols, slots, *refs):
    *row_refs, mine_ref, other_ref, sel_ref = refs
    me = lax.axis_index("seg")
    half = lax.rem(me, 2)
    first = me - half
    rows = jnp.concatenate([r[...] for r in row_refs], axis=0)
    owner = rows[:, cols : cols + 1].astype(F32).astype(jnp.int32)
    slot = rows[:, cols + 1 : cols + 2].astype(F32).astype(jnp.int32)
    rel = owner - first
    near = (rel >= 0) & (rel < 2)
    target = jnp.where(rel == half, 0, slots) + slot
    target = jnp.where(near, target, -1)
    lane = lax.broadcasted_iota(jnp.int32, (rows.shape[0], 2 * slots), 1)
    sel = (lane == target).astype(F32)
    step = own_rows
    sel_ref[...] = jnp.concatenate(
        [sel[i : i + step] for i in range(0, rows.shape[0], 2 * step)], axis=0
    ).astype(BF)
    sel = sel.astype(BF)
    picked = lax.dot_general(
        sel, rows[:, :cols], (((0,), (0,)), ((), ())), preferred_element_type=F32
    ).astype(BF)
    mine_ref[...] = picked[:slots]
    other_ref[...] = picked[slots:]


def readout_kernel(mine_ref, got_ref, norm_ref, mem_ref, out_ref, lift, read):
    slots, kv = mem_ref.shape[0], mem_ref.shape[1]
    cols = mine_ref.shape[1]
    heads = 2 * cols // DH
    group = heads // kv
    halves = both_halves(
        elu_plus(mine_ref[...].astype(F32)), elu_plus(got_ref[...].astype(F32))
    )
    for h in range(heads):
        at = (h * DH) % cols
        lift[:, h, :] = halves[h * DH // cols][:, at : at + DH]
    which = lax.broadcasted_iota(jnp.int32, (heads, DH), 0) // group
    for t in range(slots):
        row = lift[t]
        norm = jnp.zeros((heads, DH), F32)
        for k in range(kv):
            norm = jnp.where(which == k, norm_ref[t, k : k + 1, :], norm)
        denom = jnp.sum(row * norm, axis=1, keepdims=True)
        high = row.astype(BF).astype(F32)
        both = jnp.concatenate([high, row - high], axis=0).astype(BF)
        numer = jnp.zeros((heads, DH), F32)
        for k in range(kv):
            mem = mem_ref[t, k]
            mem_high = mem.astype(BF)
            mem_low = (mem - mem_high.astype(F32)).astype(BF)
            parts = jnp.concatenate([mem_high, mem_low], axis=1)
            every = jnp.dot(both, parts, preferred_element_type=F32)
            one = every[:heads, :DH] + (
                every[heads:, :DH] + every[:heads, DH:] + every[heads:, DH:]
            )
            numer = jnp.where(which == k, one, numer)
        read[t] = (numer / denom).astype(BF).astype(F32)
    for h in range(heads):
        out_ref[:, h * DH : (h + 1) * DH] = read[:, h, :].astype(BF)


def spread_kernel(sel_ref, mine_ref, other_ref, *out_refs):
    reads = jnp.concatenate([mine_ref[...], other_ref[...]], axis=0)
    rows = out_refs[0].shape[0]
    every = jnp.dot(sel_ref[...], reads, preferred_element_type=F32).astype(BF)
    for i, out in enumerate(out_refs):
        out[...] = every[i * rows : (i + 1) * rows]


def fetch_kernel(*refs):
    *refs, sems = refs
    half = len(refs) // 2
    copies = []
    for a, (src, dst) in enumerate(zip(refs[:half], refs[half:])):
        count = min(sems.shape[1], src.shape[0])
        depth = src.shape[0] // count
        for i in range(count):
            at = pl.ds(i * depth, depth)
            copies.append(pltpu.make_async_copy(src.at[at], dst.at[at], sems.at[a, i]))
    for c in copies:
        c.start()
    for c in copies:
        c.wait()


def columns_of(w_ref, tp, j):
    cols = w_ref.shape[1] // tp
    first = lax.rem(lax.axis_index("tp") + j, tp) * cols
    return w_ref[:, pl.ds(pl.multiple_of(first, DH), cols)]


def away_kernel(tp, gate_hbm, kept_ref, got_ref, local_ref, w_ref, out_ref, att_ref, gate_ref, small):
    heads = local_ref.shape[1]
    for c in fetch_all([(gate_hbm, gate_ref)], small):
        c.wait()
    gate = jax.nn.sigmoid(gate_ref[...])
    for h in range(heads):
        at = slice(h * DH, (h + 1) * DH)
        memory = kept_ref[:, at].astype(F32) + got_ref[:, at].astype(F32)
        mix = gate[:, h : h + 1]
        att_ref[:, at] = (mix * memory + (1.0 - mix) * local_ref[:, h, :]).astype(BF)
    for j in range(1, tp):
        out_ref[j - 1] = jnp.dot(
            att_ref[...], columns_of(w_ref, tp, j), preferred_element_type=F32
        ).astype(out_ref.dtype)


def home_kernel(tp, att_ref, w_ref, out_ref):
    out_ref[...] = jnp.dot(att_ref[...], columns_of(w_ref, tp, 0), preferred_element_type=F32)


def body(seg, tp, tokens, w_query, w_key, w_value, w_out, gate_bias, mem_store, norm_store,
         k_cache, v_cache, home_owner, home_slot, cache_len, win_start):
    rows, width = tokens.shape
    cols = w_query.shape[1]
    heads = cols // DH
    window = k_cache.shape[1]
    kv_cols = k_cache.shape[2]
    kv = kv_cols // DH
    slots = mem_store.shape[0]
    chips = seg // 2
    zs = chips // 2
    sds = jax.ShapeDtypeStruct
    dma = pltpu.SemaphoreType.DMA

    def swap(value, mask):
        return lax.ppermute(value, "seg", [(i, i ^ mask) for i in range(seg)])

    q_blocks = 16
    half = cols // 2
    query, give, limits = call(
        query_kernel, "query",
        [sds((2 * rows, half + DH), BF), sds((rows, half), BF), sds((8, DH), F32)],
        [HBM, HBM, ANY, ANY, HBM, HBM, HBM, ANY, HBM],
        [pltpu.SMEM((rows,), jnp.int32)] * 6
        + [pltpu.VMEM((2 * rows, width), BF),
           pltpu.VMEM((q_blocks, width // q_blocks, half), BF), dma((q_blocks,)), dma((8,))],
        16, 4 * rows * width * half, 2 * width * half,
        (home_owner, home_slot, swap(home_owner, 1), swap(home_slot, 1), cache_len, win_start,
         tokens, swap(tokens, 1), w_query),
    )
    query, give, limits, tokens_late = lax.optimization_barrier((query, give, limits, tokens))
    near = swap(query, seg // 2)
    query_got = swap(give, 1)
    kv_blocks = 8
    key_new, value_new = call(
        keyval_kernel, "keyval",
        [sds((rows, kv_cols), BF)] * 2,
        [ANY, ANY, ANY],
        [pltpu.VMEM((rows, width), BF)]
        + [pltpu.VMEM((kv_blocks, width // kv_blocks, kv_cols), BF)] * 2
        + [dma((2, kv_blocks)), dma((1,))],
        12, 4 * rows * width * kv_cols, 4 * width * kv_cols,
        (tokens_late, w_key, w_value),
    )
    near, query_got, key_new, value_new = lax.optimization_barrier(
        (near, query_got, key_new, value_new)
    )
    pair = jnp.concatenate([query, near], axis=0)
    far = [swap(pair, 2 * j) for j in range(1, zs)]
    scores, query_heads = call(
        scores_kernel, "scores",
        [sds((rows, heads, window), F32), sds((rows, heads, DH), F32)],
        [VM, VM, VM, HBM],
        [pltpu.SMEM((rows,), jnp.int32)] * 2
        + [pltpu.VMEM((rows, window, kv_cols), BF), pltpu.VMEM((rows, heads, kv_cols), BF),
           dma((rows,))],
        20, 2 * rows * heads * window * kv_cols, rows * window * kv_cols,
        (limits, query, query_got, k_cache),
    )
    far, scores, query_heads = lax.optimization_barrier((far, scores, query_heads))
    mine, other, sel = call(
        functools.partial(route_kernel, rows, half, slots), "route",
        [sds((slots, half), BF)] * 2 + [sds((chips * rows, 2 * slots), BF)],
        [VM] * zs, [], 8, 4 * slots * chips * rows * cols, 0,
        (pair, *far),
    )
    got = swap(other, 1)
    mem_fast, norm_fast = call(
        fetch_kernel, "fetch_memory",
        [sds(mem_store.shape, F32), sds(norm_store.shape, F32)],
        [ANY, ANY], [dma((2, 8))],
        4, 0, 4 * slots * kv * DH * DH,
        (mem_store, norm_store),
    )
    got, mem_fast, norm_fast = lax.optimization_barrier((got, mem_fast, norm_fast))
    read = call(
        readout_kernel, "readout",
        sds((slots, cols), BF), [VM] * 4, [pltpu.VMEM((slots, heads, DH), F32)] * 2,
        8, 8 * slots * heads * DH * DH, 0,
        (mine, got, norm_fast, mem_fast),
    )
    partner = swap(read, 1)
    probs, own_prob = call(
        probs_kernel, "probs",
        [sds((rows, heads, window), BF), sds((rows, heads, DH), F32)],
        [VM] * 4,
        [pltpu.SMEM((rows,), jnp.int32)] * 2,
        8, 20 * rows * heads * window, 0,
        (limits, query_heads, key_new, scores),
    )
    partner, probs, own_prob = lax.optimization_barrier((partner, probs, own_prob))
    here, *away = call(
        spread_kernel, "spread",
        [sds((2 * rows, cols), BF)] * zs,
        [VM] * 3, [], 8, 4 * slots * chips * rows * cols, 0,
        (sel, read, partner),
    )
    back = [swap(away[j - 1], 2 * j) for j in range(1, zs)]
    away, probs = lax.optimization_barrier((away, probs))
    local_read = call(
        values_kernel, "values",
        sds((rows, heads, DH), F32),
        [VM, VM, VM, VM, HBM],
        [pltpu.SMEM((rows,), jnp.int32)] * 2
        + [pltpu.VMEM((rows, window, kv_cols), BF), dma((rows,))],
        18, 2 * rows * heads * window * kv_cols, rows * window * kv_cols,
        (limits, probs, own_prob, value_new.reshape(rows, 1, kv_cols), v_cache),
    )
    back, local_read = lax.optimization_barrier((back, local_read))
    for value in back:
        here = here + value
    kept, leaving = here[:rows], here[rows:]
    last = swap(leaving, seg // 2)
    w_fast = call(
        fetch_kernel, "fetch",
        [sds(w_out.shape, BF)], [ANY], [dma((1, 16))],
        4, 0, 2 * w_out.shape[0] * w_out.shape[1],
        (w_out,),
    )[0]
    last, w_fast = lax.optimization_barrier((last, w_fast))
    out_cols = w_out.shape[1] // tp
    others, attended = call(
        functools.partial(away_kernel, tp), "away",
        [sds((tp - 1, rows, out_cols), F32), sds((rows, cols), BF)],
        [ANY, VM, VM, VM, VM], [pltpu.VMEM((1, heads), F32), dma((1,))],
        4, 2 * rows * cols * (w_out.shape[1] - out_cols), 0,
        (gate_bias.reshape(1, heads), kept, last, local_read, w_fast),
    )
    came = [
        lax.ppermute(others[j - 1], "tp", [(i, (i + j) % tp) for i in range(tp)])
        for j in range(1, tp)
    ]
    result = call(
        functools.partial(home_kernel, tp), "home",
        sds((rows, out_cols), F32), [VM, VM], [],
        4, 2 * rows * cols * out_cols, 0,
        (attended, w_fast),
    )
    came, result = lax.optimization_barrier((came, result))
    for value in came:
        result = result + value
    return result.astype(BF)


def solution(mesh):
    placed = (
        P("seg", None),
        P(None, "tp"),
        P(None, "tp"),
        P(None, "tp"),
        P("tp", None),
        P("tp"),
        P("seg", "tp", None, None),
        P("seg", "tp", None),
        P("seg", None, "tp"),
        P("seg", None, "tp"),
        P("seg"),
        P("seg"),
        P("seg"),
        P("seg"),
    )
    inner = functools.partial(body, mesh.shape["seg"], mesh.shape["tp"])
    return jax.shard_map(
        inner, mesh=mesh, in_specs=placed, out_specs=P("seg", "tp"), check_vma=False
    )
```

```python
import functools

import jax
import jax.numpy as jnp
from jax import lax
from jax.experimental import pallas as pl
from jax.experimental.pallas import tpu as pltpu
from jax.sharding import PartitionSpec as P

DH = 128
MIB = 2**20
STRETCHES = 8
BF = jnp.bfloat16
F32 = jnp.float32

ANY = pl.BlockSpec(memory_space=pl.ANY)
VM = pl.BlockSpec(memory_space=pltpu.VMEM)
HBM = pl.BlockSpec(memory_space=pltpu.HBM)


def call(kernel, name, out_shape, in_specs, scratch, mib, flops, nbytes, args):
    many = isinstance(out_shape, (list, tuple))
    args = [
        pltpu.with_memory_space_constraint(a, pltpu.HBM) if spec is HBM else a
        for a, spec in zip(args, in_specs)
    ]
    return pl.pallas_call(
        kernel,
        name=name,
        out_shape=out_shape,
        in_specs=in_specs,
        out_specs=[VM] * len(out_shape) if many else VM,
        scratch_shapes=scratch,
        compiler_params=pltpu.CompilerParams(vmem_limit_bytes=mib * MIB),
        cost_estimate=pl.CostEstimate(flops=flops, bytes_accessed=nbytes, transcendentals=0),
    )(*args)


def elu_plus(values):
    return jnp.where(values > 0, values + 1.0, jnp.exp(jnp.minimum(values, 0.0)))


def fetch_all(pairs, sems):
    copies = [pltpu.make_async_copy(a, b, sems.at[i]) for i, (a, b) in enumerate(pairs)]
    for c in copies:
        c.start()
    return copies


def query_kernel(owner_hbm, slot_hbm, owner2_hbm, slot2_hbm, len_hbm, start_hbm, x_hbm, x2_hbm, w_ref,
                 q_ref, give_ref, limit_ref, owner_ref, slot_ref, owner2_ref, slot2_ref, len_ref,
                 start_ref, x_ref, buf, sems, small):
    rows = x_hbm.shape[0]
    count, depth, cols = buf.shape
    first = pl.multiple_of(lax.rem(lax.axis_index("seg"), 2) * cols, DH)

    def copy(i):
        at = pl.ds(i * depth, depth)
        return pltpu.make_async_copy(w_ref.at[at, pl.ds(first, cols)], buf.at[i], sems.at[i])

    ready = fetch_all(
        [(x_hbm, x_ref.at[:rows]), (x2_hbm, x_ref.at[rows:]), (owner_hbm, owner_ref),
         (slot_hbm, slot_ref), (owner2_hbm, owner2_ref), (slot2_hbm, slot2_ref),
         (len_hbm, len_ref), (start_hbm, start_ref)],
        small,
    )
    for i in range(count):
        copy(i).start()
    for c in ready:
        c.wait()
    row = lax.broadcasted_iota(jnp.int32, (2 * rows, DH), 0)
    lane = lax.broadcasted_iota(jnp.int32, (2 * rows, DH), 1)
    extra = jnp.zeros((2 * rows, DH), F32)
    for r in range(rows):
        for at, one, two in ((r, owner_ref, slot_ref), (rows + r, owner2_ref, slot2_ref)):
            extra = jnp.where((row == at) & (lane == 0), one[r].astype(F32), extra)
            extra = jnp.where((row == at) & (lane == 1), two[r].astype(F32), extra)
    q_ref[:, cols:] = extra.astype(BF)
    row = lax.broadcasted_iota(jnp.int32, limit_ref.shape, 0)
    lane = lax.broadcasted_iota(jnp.int32, limit_ref.shape, 1)
    limit = jnp.zeros(limit_ref.shape, F32)
    for r in range(rows):
        ends = jnp.where(row == 0, len_ref[r].astype(F32), start_ref[r].astype(F32))
        limit = jnp.where(lane == r, ends, limit)
    limit_ref[...] = limit
    total = jnp.zeros((2 * rows, cols), F32)
    for i in range(count):
        copy(i).wait()
        total = total + jnp.dot(
            x_ref[:, i * depth : (i + 1) * depth], buf[i], preferred_element_type=F32
        )
    q_ref[:, :cols] = total.astype(BF)
    give_ref[...] = total[rows:].astype(BF)


def read_limits(limit_ref, len_ref, start_ref):
    shape = (1, limit_ref.shape[1])
    lane = lax.broadcasted_iota(jnp.int32, shape, 1)
    for r in range(len_ref.shape[0]):
        for i, out in enumerate((len_ref, start_ref)):
            one = jnp.where(lane == r, limit_ref[i : i + 1, :], 0.0)
            out[r] = jnp.sum(one).astype(jnp.int32)


def both_halves(own, got):
    even = lax.rem(lax.axis_index("seg"), 2) == 0
    return jnp.where(even, own, got), jnp.where(even, got, own)


def keyval_kernel(x_hbm, wk_ref, wv_ref, k_ref, v_ref, x_ref, bufk, bufv, sems, small):
    count, depth = bufk.shape[0], bufk.shape[1]

    def copies(i):
        at = pl.ds(i * depth, depth)
        return (
            pltpu.make_async_copy(wk_ref.at[at, :], bufk.at[i], sems.at[0, i]),
            pltpu.make_async_copy(wv_ref.at[at, :], bufv.at[i], sems.at[1, i]),
        )

    first = fetch_all([(x_hbm, x_ref)], small)
    for i in range(count):
        for c in copies(i):
            c.start()
    first[0].wait()
    key = jnp.zeros(k_ref.shape, F32)
    val = jnp.zeros(v_ref.shape, F32)
    for i in range(count):
        for c in copies(i):
            c.wait()
        part = x_ref[:, i * depth : (i + 1) * depth]
        key = key + jnp.dot(part, bufk[i], preferred_element_type=F32)
        val = val + jnp.dot(part, bufv[i], preferred_element_type=F32)
    k_ref[...] = key.astype(BF)
    v_ref[...] = val.astype(BF)


def live_blocks(start_ref, len_ref, r):
    lo = start_ref[r] // DH
    return lo, jnp.maximum((len_ref[r] + DH - 1) // DH - lo, 0)


def each_copy(cache_ref, buf, sems, r, lo, count, act):
    size = 1
    while size < buf.shape[1] // DH:
        size *= 2
    while size:
        here, now = lo, size

        @pl.when((count & now) != 0)
        def _():
            at = pl.ds(pl.multiple_of(here * DH, DH), now * DH)
            act(pltpu.make_async_copy(cache_ref.at[r, at, :], buf.at[r, at, :], sems.at[r]))

        lo = lo + (count & size)
        size //= 2


def by_length(window, lo, count, step, act):
    need = (count * DH + step - 1) // step
    for n in range(1, window // step + 1):
        first = pl.multiple_of(jnp.minimum(lo * DH, window - n * step), DH)
        pl.when(need == n)(functools.partial(act, first, n * step))


def scores_kernel(limit_ref, own_ref, got_ref, kc_ref, score_ref, qh_ref, len_ref, start_ref,
                  buf, wide_ref, sems):
    rows, heads, window = score_ref.shape
    kv = kc_ref.shape[2] // DH
    group = heads // kv
    read_limits(limit_ref, len_ref, start_ref)

    @pl.loop(0, rows)
    def _(r):
        lo, count = live_blocks(start_ref, len_ref, r)
        each_copy(kc_ref, buf, sems, r, lo, count, lambda c: c.start())

    cols = got_ref.shape[1]
    halves = both_halves(own_ref[:rows, :cols].astype(F32), got_ref[...].astype(F32))
    for h in range(heads):
        at = (h * DH) % cols
        qh_ref[:, h, :] = halves[h * DH // cols][:, at : at + DH]
    which = lax.broadcasted_iota(jnp.int32, (heads, DH), 0) // group
    for r in range(rows):
        q = qh_ref[r]
        for k in range(kv):
            wide_ref[r, :, k * DH : (k + 1) * DH] = jnp.where(which == k, q, 0.0).astype(BF)

    @pl.loop(0, rows)
    def _(r):
        lo, count = live_blocks(start_ref, len_ref, r)
        each_copy(kc_ref, buf, sems, r, lo, count, lambda c: c.wait())

        def product(first, size):
            at = pl.ds(first, size)
            score_ref[r, :, at] = lax.dot_general(
                wide_ref[r], buf[r, at, :], (((1,), (1,)), ((), ())), preferred_element_type=F32
            )

        by_length(window, lo, count, window // STRETCHES, product)


def probs_kernel(limit_ref, qh_ref, kn_ref, score_ref, p_ref, own_ref, len_ref, start_ref):
    rows, heads, window = p_ref.shape
    kv = kn_ref.shape[1] // DH
    group = heads // kv
    read_limits(limit_ref, len_ref, start_ref)
    which = lax.broadcasted_iota(jnp.int32, (heads, DH), 0) // group
    position = lax.broadcasted_iota(jnp.int32, (heads, window), 1)
    scale = DH ** (-0.5)
    for r in range(rows):
        q = qh_ref[r]
        key = jnp.zeros((heads, DH), F32)
        for k in range(kv):
            one = kn_ref[r : r + 1, k * DH : (k + 1) * DH].astype(F32)
            key = jnp.where(which == k, one, key)
        own = jnp.sum(q * key, axis=1, keepdims=True) * scale
        live = (position >= start_ref[r]) & (position < len_ref[r])
        s = jnp.where(live, score_ref[r] * scale, -jnp.inf)
        top = jnp.maximum(jnp.max(s, axis=1, keepdims=True), own)
        weight = jnp.exp(s - top)
        own_weight = jnp.exp(own - top)
        inverse = 1.0 / (jnp.sum(weight, axis=1, keepdims=True) + own_weight)
        p_ref[r] = (weight * inverse).astype(BF)
        prob = (own_weight * inverse).astype(BF).astype(F32)
        own_ref[r] = jnp.broadcast_to(prob, (heads, DH))


def values_kernel(limit_ref, p_ref, own_ref, vn_ref, vc_ref, out_ref, len_ref, start_ref,
                  buf, sems):
    rows, heads, window = p_ref.shape
    kv = vc_ref.shape[2] // DH
    group = heads // kv
    read_limits(limit_ref, len_ref, start_ref)

    @pl.loop(0, rows)
    def _(r):
        lo, count = live_blocks(start_ref, len_ref, r)
        each_copy(vc_ref, buf, sems, r, lo, count, lambda c: c.start())

    which = lax.broadcasted_iota(jnp.int32, (heads, DH), 0) // group
    nothing = jnp.zeros((DH, kv * DH), BF)

    @pl.loop(0, rows)
    def _(r):
        lo, count = live_blocks(start_ref, len_ref, r)
        base = jnp.zeros((heads, DH), F32)
        for k in range(kv):
            value = vn_ref[r, :, k * DH : (k + 1) * DH].astype(F32)
            base = jnp.where(which == k, own_ref[r] * value, base)
        out_ref[r] = base

        def clear(b):
            buf[r, pl.ds(pl.multiple_of(b * DH, DH), DH), :] = nothing

        def product(first, size):
            pl.loop(first // DH, lo)(clear)
            pl.loop(lo + count, (first + size) // DH)(clear)
            each_copy(vc_ref, buf, sems, r, lo, count, lambda c: c.wait())
            at = pl.ds(first, size)
            every = jnp.dot(p_ref[r, :, at], buf[r, at, :], preferred_element_type=F32)
            read = jnp.zeros((heads, DH), F32)
            for k in range(kv):
                read = jnp.where(which == k, every[:, k * DH : (k + 1) * DH], read)
            out_ref[r] += read

        by_length(window, lo, count, window // STRETCHES, product)


def route_kernel(own_rows, cols, slots, *refs):
    *row_refs, mine_ref, other_ref, sel_ref = refs
    me = lax.axis_index("seg")
    half = lax.rem(me, 2)
    first = me - half
    rows = jnp.concatenate([r[...] for r in row_refs], axis=0)
    owner = rows[:, cols : cols + 1].astype(F32).astype(jnp.int32)
    slot = rows[:, cols + 1 : cols + 2].astype(F32).astype(jnp.int32)
    rel = owner - first
    near = (rel >= 0) & (rel < 2)
    target = jnp.where(rel == half, 0, slots) + slot
    target = jnp.where(near, target, -1)
    lane = lax.broadcasted_iota(jnp.int32, (rows.shape[0], 2 * slots), 1)
    sel = (lane == target).astype(F32)
    step = own_rows
    sel_ref[...] = jnp.concatenate(
        [sel[i : i + step] for i in range(0, rows.shape[0], 2 * step)], axis=0
    ).astype(BF)
    sel = sel.astype(BF)
    picked = lax.dot_general(
        sel, rows[:, :cols], (((0,), (0,)), ((), ())), preferred_element_type=F32
    ).astype(BF)
    mine_ref[...] = picked[:slots]
    other_ref[...] = picked[slots:]


def readout_kernel(mine_ref, got_ref, norm_ref, mem_ref, out_ref, lift, read):
    slots, kv = mem_ref.shape[0], mem_ref.shape[1]
    cols = mine_ref.shape[1]
    heads = 2 * cols // DH
    group = heads // kv
    halves = both_halves(
        elu_plus(mine_ref[...].astype(F32)), elu_plus(got_ref[...].astype(F32))
    )
    for h in range(heads):
        at = (h * DH) % cols
        lift[:, h, :] = halves[h * DH // cols][:, at : at + DH]
    which = lax.broadcasted_iota(jnp.int32, (heads, DH), 0) // group
    for t in range(slots):
        row = lift[t]
        norm = jnp.zeros((heads, DH), F32)
        for k in range(kv):
            norm = jnp.where(which == k, norm_ref[t, k : k + 1, :], norm)
        denom = jnp.sum(row * norm, axis=1, keepdims=True)
        high = row.astype(BF).astype(F32)
        both = jnp.concatenate([high, row - high], axis=0).astype(BF)
        numer = jnp.zeros((heads, DH), F32)
        for k in range(kv):
            mem = mem_ref[t, k]
            mem_high = mem.astype(BF)
            mem_low = (mem - mem_high.astype(F32)).astype(BF)
            parts = jnp.concatenate([mem_high, mem_low], axis=1)
            every = jnp.dot(both, parts, preferred_element_type=F32)
            one = every[:heads, :DH] + (
                every[heads:, :DH] + every[:heads, DH:] + every[heads:, DH:]
            )
            numer = jnp.where(which == k, one, numer)
        read[t] = (numer / denom).astype(BF).astype(F32)
    for h in range(heads):
        out_ref[:, h * DH : (h + 1) * DH] = read[:, h, :].astype(BF)


def spread_kernel(sel_ref, mine_ref, other_ref, *out_refs):
    reads = jnp.concatenate([mine_ref[...], other_ref[...]], axis=0)
    rows = out_refs[0].shape[0]
    every = jnp.dot(sel_ref[...], reads, preferred_element_type=F32).astype(BF)
    for i, out in enumerate(out_refs):
        out[...] = every[i * rows : (i + 1) * rows]


def fetch_kernel(*refs):
    *refs, sems = refs
    half = len(refs) // 2
    copies = []
    for a, (src, dst) in enumerate(zip(refs[:half], refs[half:])):
        count = min(sems.shape[1], src.shape[0])
        depth = src.shape[0] // count
        for i in range(count):
            at = pl.ds(i * depth, depth)
            copies.append(pltpu.make_async_copy(src.at[at], dst.at[at], sems.at[a, i]))
    for c in copies:
        c.start()
    for c in copies:
        c.wait()


def columns_of(w_ref, tp, j):
    cols = w_ref.shape[1] // tp
    first = lax.rem(lax.axis_index("tp") + j, tp) * cols
    return w_ref[:, pl.ds(pl.multiple_of(first, DH), cols)]


def away_kernel(tp, gate_hbm, kept_ref, got_ref, local_ref, w_ref, out_ref, att_ref, gate_ref, small):
    heads = local_ref.shape[1]
    for c in fetch_all([(gate_hbm, gate_ref)], small):
        c.wait()
    gate = jax.nn.sigmoid(gate_ref[...])
    for h in range(heads):
        at = slice(h * DH, (h + 1) * DH)
        memory = kept_ref[:, at].astype(F32) + got_ref[:, at].astype(F32)
        mix = gate[:, h : h + 1]
        att_ref[:, at] = (mix * memory + (1.0 - mix) * local_ref[:, h, :]).astype(BF)
    for j in range(1, tp):
        out_ref[j - 1] = jnp.dot(
            att_ref[...], columns_of(w_ref, tp, j), preferred_element_type=F32
        ).astype(out_ref.dtype)


def home_kernel(tp, att_ref, w_ref, out_ref):
    out_ref[...] = jnp.dot(att_ref[...], columns_of(w_ref, tp, 0), preferred_element_type=F32)


def body(seg, tp, tokens, w_query, w_key, w_value, w_out, gate_bias, mem_store, norm_store,
         k_cache, v_cache, home_owner, home_slot, cache_len, win_start):
    rows, width = tokens.shape
    cols = w_query.shape[1]
    heads = cols // DH
    window = k_cache.shape[1]
    kv_cols = k_cache.shape[2]
    kv = kv_cols // DH
    slots = mem_store.shape[0]
    chips = seg // 2
    zs = chips // 2
    sds = jax.ShapeDtypeStruct
    dma = pltpu.SemaphoreType.DMA

    def swap(value, mask):
        return lax.ppermute(value, "seg", [(i, i ^ mask) for i in range(seg)])

    q_blocks = 32
    half = cols // 2
    query, give, limits = call(
        query_kernel, "query",
        [sds((2 * rows, half + DH), BF), sds((rows, half), BF), sds((8, DH), F32)],
        [HBM, HBM, ANY, ANY, HBM, HBM, HBM, ANY, HBM],
        [pltpu.SMEM((rows,), jnp.int32)] * 6
        + [pltpu.VMEM((2 * rows, width), BF),
           pltpu.VMEM((q_blocks, width // q_blocks, half), BF), dma((q_blocks,)), dma((8,))],
        16, 4 * rows * width * half, 2 * width * half,
        (home_owner, home_slot, swap(home_owner, 1), swap(home_slot, 1), cache_len, win_start,
         tokens, swap(tokens, 1), w_query),
    )
    query, give, limits, tokens_late = lax.optimization_barrier((query, give, limits, tokens))
    near = swap(query, seg // 2)
    query_got = swap(give, 1)
    kv_blocks = 8
    key_new, value_new = call(
        keyval_kernel, "keyval",
        [sds((rows, kv_cols), BF)] * 2,
        [ANY, ANY, ANY],
        [pltpu.VMEM((rows, width), BF)]
        + [pltpu.VMEM((kv_blocks, width // kv_blocks, kv_cols), BF)] * 2
        + [dma((2, kv_blocks)), dma((1,))],
        12, 4 * rows * width * kv_cols, 4 * width * kv_cols,
        (tokens_late, w_key, w_value),
    )
    near, query_got, key_new, value_new = lax.optimization_barrier(
        (near, query_got, key_new, value_new)
    )
    pair = jnp.concatenate([query, near], axis=0)
    far = [swap(pair, 2 * j) for j in range(1, zs)]
    scores, query_heads = call(
        scores_kernel, "scores",
        [sds((rows, heads, window), F32), sds((rows, heads, DH), F32)],
        [VM, VM, VM, HBM],
        [pltpu.SMEM((rows,), jnp.int32)] * 2
        + [pltpu.VMEM((rows, window, kv_cols), BF), pltpu.VMEM((rows, heads, kv_cols), BF),
           dma((rows,))],
        20, 2 * rows * heads * window * kv_cols, rows * window * kv_cols,
        (limits, query, query_got, k_cache),
    )
    far, scores, query_heads = lax.optimization_barrier((far, scores, query_heads))
    mine, other, sel = call(
        functools.partial(route_kernel, rows, half, slots), "route",
        [sds((slots, half), BF)] * 2 + [sds((chips * rows, 2 * slots), BF)],
        [VM] * zs, [], 8, 4 * slots * chips * rows * cols, 0,
        (pair, *far),
    )
    got = swap(other, 1)
    mem_fast, norm_fast = call(
        fetch_kernel, "fetch_memory",
        [sds(mem_store.shape, F32), sds(norm_store.shape, F32)],
        [ANY, ANY], [dma((2, 8))],
        4, 0, 4 * slots * kv * DH * DH,
        (mem_store, norm_store),
    )
    got, mem_fast, norm_fast = lax.optimization_barrier((got, mem_fast, norm_fast))
    read = call(
        readout_kernel, "readout",
        sds((slots, cols), BF), [VM] * 4, [pltpu.VMEM((slots, heads, DH), F32)] * 2,
        8, 8 * slots * heads * DH * DH, 0,
        (mine, got, norm_fast, mem_fast),
    )
    partner = swap(read, 1)
    probs, own_prob = call(
        probs_kernel, "probs",
        [sds((rows, heads, window), BF), sds((rows, heads, DH), F32)],
        [VM] * 4,
        [pltpu.SMEM((rows,), jnp.int32)] * 2,
        8, 20 * rows * heads * window, 0,
        (limits, query_heads, key_new, scores),
    )
    partner, probs, own_prob = lax.optimization_barrier((partner, probs, own_prob))
    here, *away = call(
        spread_kernel, "spread",
        [sds((2 * rows, cols), BF)] * zs,
        [VM] * 3, [], 8, 4 * slots * chips * rows * cols, 0,
        (sel, read, partner),
    )
    back = [swap(away[j - 1], 2 * j) for j in range(1, zs)]
    away, probs = lax.optimization_barrier((away, probs))
    local_read = call(
        values_kernel, "values",
        sds((rows, heads, DH), F32),
        [VM, VM, VM, VM, HBM],
        [pltpu.SMEM((rows,), jnp.int32)] * 2
        + [pltpu.VMEM((rows, window, kv_cols), BF), dma((rows,))],
        18, 2 * rows * heads * window * kv_cols, rows * window * kv_cols,
        (limits, probs, own_prob, value_new.reshape(rows, 1, kv_cols), v_cache),
    )
    back, local_read = lax.optimization_barrier((back, local_read))
    for value in back:
        here = here + value
    kept, leaving = here[:rows], here[rows:]
    last = swap(leaving, seg // 2)
    w_fast = call(
        fetch_kernel, "fetch",
        [sds(w_out.shape, BF)], [ANY], [dma((1, 16))],
        4, 0, 2 * w_out.shape[0] * w_out.shape[1],
        (w_out,),
    )[0]
    last, w_fast = lax.optimization_barrier((last, w_fast))
    out_cols = w_out.shape[1] // tp
    others, attended = call(
        functools.partial(away_kernel, tp), "away",
        [sds((tp - 1, rows, out_cols), F32), sds((rows, cols), BF)],
        [ANY, VM, VM, VM, VM], [pltpu.VMEM((1, heads), F32), dma((1,))],
        4, 2 * rows * cols * (w_out.shape[1] - out_cols), 0,
        (gate_bias.reshape(1, heads), kept, last, local_read, w_fast),
    )
    came = [
        lax.ppermute(others[j - 1], "tp", [(i, (i + j) % tp) for i in range(tp)])
        for j in range(1, tp)
    ]
    result = call(
        functools.partial(home_kernel, tp), "home",
        sds((rows, out_cols), F32), [VM, VM], [],
        4, 2 * rows * cols * out_cols, 0,
        (attended, w_fast),
    )
    came, result = lax.optimization_barrier((came, result))
    for value in came:
        result = result + value
    return result.astype(BF)


def solution(mesh):
    placed = (
        P("seg", None),
        P(None, "tp"),
        P(None, "tp"),
        P(None, "tp"),
        P("tp", None),
        P("tp"),
        P("seg", "tp", None, None),
        P("seg", "tp", None),
        P("seg", None, "tp"),
        P("seg", None, "tp"),
        P("seg"),
        P("seg"),
        P("seg"),
        P("seg"),
    )
    inner = functools.partial(body, mesh.shape["seg"], mesh.shape["tp"])
    return jax.shard_map(
        inner, mesh=mesh, in_specs=placed, out_specs=P("seg", "tp"), check_vma=False
    )
```
